512 devices in a mesh: region: 32 (over x, z), batch: 16 (over y, core).
Axes of the slice: x: 4, y: 8, z: 8, core: 2. Of those that a mesh axis runs over, the one named last changes fastest.
Arguments:
- basis_values: bfloat16 [128, 2, 4096, 512], P('region', None, 'batch'), may hold values from -6 to 6
- dens_tiles: bfloat16 [128, 512, 512], P('region', 'batch'), may hold values from -0.005859375 to 0.005859375
- region_tiles: int32 [128, 3], replicated, may hold values from 0 to 127, as said below
- point_counts: int32 [128, 16], P('region', 'batch'), may hold values from 64 to 256, as said below
- point_weights: float32 [128, 4096], P('region', 'batch'), may hold values from 0.0078125 to 0.03125
Outputs:
- xc_tiles: float32 [128, 512, 512], P('region', 'batch')
The draws below stay inside these ranges and needn't reach their ends.
Inputs may be any that keep to these rules, and one draw needn't show every extreme that they name: `region_tiles`: tile t is stored on index t // 4 of region. Regions 4 * i to 4 * i + 3 lie on index i; among their 12 entries no owner index holds more than 1 and some owner holds exactly 1, on every index; the entries of one owner on one index are different tiles. `point_counts`: every region has at least one batch with all 256 points live.
All inputs are finite; a program needn't handle non-finite values.
Results may differ from the reference program's by a relative error of at most 0.004.
Values may be sent and summed in bfloat16 or wider, within the bound.
A program may use at most 64 MiB of HBM per device.

```python
import math
import jax
import jax.numpy as jnp
from jax import lax

B = 512
POINTS = 256
REG_DEV = 4
TILE_DEV = 4
BATCHES = 16
REGIONS = 128
TILES = 128
PTS_REG = 4096


def draw_region_tiles(key, part):
    device_count = REGIONS // REG_DEV
    per_device = 3 * REG_DEV

    def one_device(sub):
        keys = jax.random.split(sub, 3)
        shuffled = jax.random.permutation(keys[0], device_count)
        offsets = jax.random.randint(keys[1], (device_count,), 0, TILE_DEV)
        position = jnp.arange(per_device)
        owners = shuffled[position % device_count]
        occurrence = position // device_count
        local_ids = (offsets[owners] + occurrence) % TILE_DEV
        tiles = owners * TILE_DEV + local_ids
        order = jax.random.permutation(keys[2], per_device)
        return tiles[order]
    device_ids = jnp.arange(device_count)
    rows = jax.vmap(lambda i: one_device(jax.random.fold_in(key, i)))(device_ids)
    return rows.reshape(REGIONS, 3).astype(jnp.int32)


def draw_point_counts(key, part):
    first_key, second_key = jax.random.split(key)
    counts = jax.random.randint(first_key, (REGIONS, BATCHES), POINTS // 4, POINTS + 1)
    full_batch = jax.random.randint(second_key, (REGIONS, 1), 0, BATCHES)
    batch_ids = jnp.arange(BATCHES)[None, :]
    return jnp.where(batch_ids == full_batch, POINTS, counts).astype(jnp.int32)


def steps_of(rng, extent, pieces, smallest, top_value):
    level = 1.0
    for dim, parts in pieces:
        steps = jax.random.uniform(jax.random.fold_in(jax.random.fold_in(rng, 6), dim), (parts,), jnp.float32, smallest / len(pieces), top_value / len(pieces))
        level = level * jnp.repeat(jnp.exp(steps), extent[dim] // parts).reshape((-1,) + (1,) * (len(extent) - 1 - dim))
    return level


def noise(stream_key, extent, deviation, most, cuts=(), kind=jnp.bfloat16):
    factor_of = steps_of(stream_key, extent, cuts, -0.22, 0.18) if cuts else 1.0
    entries = jax.random.normal(stream_key, extent, jnp.float32) * deviation * factor_of
    return jnp.minimum(jnp.maximum(entries, -most), most).astype(kind)


def setup_inputs(seed: int = 0) -> dict:
    arg_keys = jax.random.split(jax.random.key(seed), 6)
    return {
        "basis_values": noise(arg_keys[0], (REGIONS, 2, PTS_REG, B), 1.0, 6.0, ((0, 32), (2, 16))),
        "dens_tiles": noise(arg_keys[1], (TILES, B, B), (0.5 / B), 0.005859375, ((0, 32), (1, 16))),
        "region_tiles": draw_region_tiles(jax.random.fold_in(arg_keys[5], 71), 0),
        "point_counts": draw_point_counts(jax.random.fold_in(arg_keys[5], 71), 0),
        "point_weights": jnp.clip(jnp.exp(math.log(0.03125) - 1.3862944 * jax.random.uniform(arg_keys[4], (REGIONS, PTS_REG), jnp.float32) ** steps_of(arg_keys[4], (REGIONS, PTS_REG), ((0, 32), (1, 16)), -0.2, 0.2)), 0.0078125, 0.03125),
    }


SLATER = 0.9847450218426964


def potential(density):
    return -SLATER * density * jnp.power(density * density + 1.0, -1.0 / 3.0)


def batch_partial(left, right, block_width):
    left_parts = left.astype(jnp.float32).reshape(BATCHES, POINTS, block_width)
    right_parts = right.astype(jnp.float32).reshape(BATCHES, POINTS, block_width)
    terms = jnp.einsum("npi,npj->nij", left_parts, right_parts)
    rounded = lax.optimization_barrier(terms.astype(jnp.bfloat16))
    return jnp.sum(rounded.astype(jnp.float32), axis=0)


def reference(basis_values, dens_tiles, region_tiles, point_counts, point_weights):
    block_width = dens_tiles.shape[1]
    position = jnp.arange(PTS_REG, dtype=jnp.int32)
    in_batch = position % POINTS
    batch_of = position // POINTS

    def region_step(totals, index):
        values = basis_values[index]
        phi_a = values[0]
        phi_b = values[1]
        tile_ids = region_tiles[index]
        tiles = dens_tiles[tile_ids]
        left_aa = jnp.dot(phi_a, tiles[0], preferred_element_type=jnp.float32)
        left_ab = jnp.dot(phi_a, tiles[1], preferred_element_type=jnp.float32)
        left_bb = jnp.dot(phi_b, tiles[2], preferred_element_type=jnp.float32)
        fa = phi_a.astype(jnp.float32)
        fb = phi_b.astype(jnp.float32)
        density = jnp.sum(fa * left_aa, axis=-1) + 2.0 * jnp.sum(fb * left_ab, axis=-1) + jnp.sum(fb * left_bb, axis=-1)
        live = in_batch < point_counts[index][batch_of]
        scale = jnp.where(live, point_weights[index] * potential(density), 0.0)
        scaled_a = (scale[:, None] * fa).astype(jnp.bfloat16)
        scaled_b = (scale[:, None] * fb).astype(jnp.bfloat16)
        pairs = jnp.stack([batch_partial(phi_a, scaled_a, block_width),
                           batch_partial(phi_a, scaled_b, block_width),
                           batch_partial(phi_b, scaled_b, block_width)])
        return totals.at[tile_ids].add(pairs), None

    start_sums = jnp.zeros(dens_tiles.shape, jnp.float32)
    result, _ = lax.scan(region_step, start_sums, jnp.arange(REGIONS, dtype=jnp.int32))
    return result
```

```python
import functools

import jax
import jax.numpy as jnp
from jax import lax
from jax.experimental import pallas as pl
from jax.experimental.pallas import tpu as pltpu
from jax.sharding import PartitionSpec as P

SLATER = 0.9847450218426964
MESH = pl.DeviceIdType.MESH


def potential(density):
    return -SLATER * density * jnp.exp(jnp.log(density * density + 1.0) * (-1.0 / 3.0))


def batch_kernel(
    ring, far, regions, rows, own_ref, phi_ref, weight_ref, out_ref,
    tiles, pairs, peer, sum_up, got_up, sum_down, got_down,
    up_send, up_recv, down_send, down_recv, side_send, side_recv,
    swap_send, swap_recv, red_up_send, red_up_recv, red_down_send, red_down_recv,
):
    near = ring - 1 - far
    me = lax.axis_index("batch")
    y, c = me // 2, me % 2
    way = 1 - 2 * c
    other = y * 2 + (1 - c)

    def at(k):
        return lax.rem(y + k * way + ring, ring)

    def mine(k):
        return at(k) * 2 + c

    def theirs(k):
        return at(k) * 2 + (1 - c)

    barrier = pltpu.get_barrier_semaphore()
    for target in (mine(1), mine(-1), other):
        pl.semaphore_signal(barrier, inc=1, device_id={"batch": target}, device_id_type=MESH)
    pl.semaphore_wait(barrier, 3)

    def remote(src, dst, send, recv, target):
        return pltpu.make_async_remote_copy(
            src_ref=src, dst_ref=dst, send_sem=send, recv_sem=recv,
            device_id={"batch": target}, device_id_type=MESH,
        )

    def part(r):
        return pl.ds(3 * r, 3)

    def block(r, slot):
        return tiles.at[part(r), slot]

    def up_hop(a, r):
        src = own_ref.at[part(r)] if a == 0 else block(r, mine(-a))
        return remote(src, block(r, mine(-a)), up_send.at[a, r], up_recv.at[a, r], mine(1))

    def up_arrival(a, r):
        slot = block(r, mine(-(a + 1)))
        return remote(slot, slot, up_send.at[a, r], up_recv.at[a, r], mine(1))

    def down_hop(a, r):
        src = own_ref.at[part(r)] if a == 0 else block(r, mine(a))
        return remote(src, block(r, mine(a)), down_send.at[a, r], down_recv.at[a, r], mine(-1))

    def down_arrival(a, r):
        slot = block(r, mine(a + 1))
        return remote(slot, slot, down_send.at[a, r], down_recv.at[a, r], mine(-1))

    def side(i, r):
        if i == 0:
            src, slot = own_ref.at[part(r)], block(r, me)
        else:
            slot = block(r, mine(-i if i <= far else i - far))
            src = slot
        return remote(src, slot, side_send.at[i, r], side_recv.at[i, r], other)

    def side_arrival(i, r):
        k = 0 if i == 0 else (i if i <= far else far - i)
        slot = block(r, theirs(k))
        return remote(slot, slot, side_send.at[i, r], side_recv.at[i, r], other)

    def gather_step(a, r):
        if a == 0:
            up_hop(0, r).start()
            down_hop(0, r).start()
            side(0, r).start()
            tiles[part(r), me] = own_ref[part(r)]
            return
        up_arrival(a - 1, r).wait_recv()
        if a < far:
            up_hop(a, r).start()
        side(a, r).start()
        if a <= near:
            down_arrival(a - 1, r).wait_recv()
            if a < near:
                down_hop(a, r).start()
            side(far + a, r).start()

    def swap(r):
        return remote(
            pairs.at[part(r), :, 1 - c], peer.at[part(r)],
            swap_send.at[r], swap_recv.at[r], other,
        )

    def compute(r):
        for i in range(ring):
            side_arrival(i, r).wait_recv()
        width = phi_ref.shape[-1]
        phi_a, phi_b = phi_ref[r, 0], phi_ref[r, 1]

        def left(values, j):
            matrix = tiles[3 * r + j].reshape(2 * ring * rows, width)
            return jnp.dot(values, matrix, preferred_element_type=jnp.float32)

        wide_a, wide_b = phi_a.astype(jnp.float32), phi_b.astype(jnp.float32)
        density = jnp.sum(
            wide_a * left(phi_a, 0) + wide_b * (2.0 * left(phi_a, 1) + left(phi_b, 2)),
            axis=1, keepdims=True,
        )
        scale = weight_ref[r] * potential(density)
        scaled_a = (scale * wide_a).astype(jnp.bfloat16)
        scaled_b = (scale * wide_b).astype(jnp.bfloat16)
        for j, (lhs, rhs) in enumerate(((phi_a, scaled_a), (phi_a, scaled_b), (phi_b, scaled_b))):
            product = lax.dot_general(
                lhs, rhs, (((0,), (0,)), ((), ())), preferred_element_type=jnp.float32
            )
            pairs[3 * r + j] = product.astype(jnp.bfloat16).reshape(ring, 2, rows, width)
        swap(r).start()

    def chip_sum(r, k):
        return pairs[part(r), at(k), c].astype(jnp.float32) + peer[part(r), at(k)].astype(jnp.float32)

    def red_up(s, r):
        return remote(
            sum_up.at[s, part(r)], got_up.at[s, part(r)],
            red_up_send.at[s, r], red_up_recv.at[s, r], mine(1),
        )

    def red_down(s, r):
        return remote(
            sum_down.at[s, part(r)], got_down.at[s, part(r)],
            red_down_send.at[s, r], red_down_recv.at[s, r], mine(-1),
        )

    def reduce_step(s, r):
        if s == 0:
            swap(r).wait_recv()
        total = chip_sum(r, far - s)
        if s > 0:
            red_up(s - 1, r).wait_recv()
            total = total + got_up[s - 1, part(r)].astype(jnp.float32)
        sum_up[s, part(r)] = total.astype(jnp.bfloat16)
        red_up(s, r).start()
        if s < near:
            total = chip_sum(r, s - near)
            if s > 0:
                red_down(s - 1, r).wait_recv()
                total = total + got_down[s - 1, part(r)].astype(jnp.float32)
            sum_down[s, part(r)] = total.astype(jnp.bfloat16)
            red_down(s, r).start()

    def finish(r):
        red_up(far - 1, r).wait_recv()
        red_down(near - 1, r).wait_recv()
        total = chip_sum(r, 0)
        total = total + got_up[far - 1, part(r)].astype(jnp.float32)
        total = total + got_down[near - 1, part(r)].astype(jnp.float32)
        out_ref[part(r)] = total.astype(out_ref.dtype)

    last = 2 * far + 2
    for r in range(regions):
        gather_step(0, r)
    for t in range(1, last + regions):
        for r in range(regions):
            stage = t - r
            if 1 <= stage <= far:
                gather_step(stage, r)
            elif far + 2 <= stage < last:
                reduce_step(stage - far - 2, r)
            elif stage == last:
                finish(r)
        if 0 <= t - far - 1 < regions:
            compute(t - far - 1)

    for r in range(regions):
        for a in range(far):
            up_hop(a, r).wait_send()
            red_up(a, r).wait_send()
        for a in range(near):
            down_hop(a, r).wait_send()
            red_down(a, r).wait_send()
        for i in range(ring):
            side(i, r).wait_send()
        swap(r).wait_send()


def over_batch(fetched, basis_values, weights, batch_count):
    ring = batch_count // 2
    far = ring // 2
    near = ring - 1 - far
    regions = basis_values.shape[0]
    requests, rows, width = fetched.shape
    dma = pltpu.SemaphoreType.DMA
    half = jnp.bfloat16
    vmem = pl.BlockSpec(memory_space=pltpu.VMEM)
    return pl.pallas_call(
        functools.partial(batch_kernel, ring, far, regions, rows),
        out_shape=jax.ShapeDtypeStruct((requests, rows, width), half),
        in_specs=[vmem] * 3,
        out_specs=vmem,
        scratch_shapes=[
            pltpu.VMEM((requests, batch_count, rows, width), half),
            pltpu.VMEM((requests, ring, 2, rows, width), half),
            pltpu.VMEM((requests, ring, rows, width), half),
            pltpu.VMEM((far, requests, rows, width), half),
            pltpu.VMEM((far, requests, rows, width), half),
            pltpu.VMEM((near, requests, rows, width), half),
            pltpu.VMEM((near, requests, rows, width), half),
            dma((far, regions)), dma((far, regions)),
            dma((near, regions)), dma((near, regions)),
            dma((ring, regions)), dma((ring, regions)),
            dma((regions,)), dma((regions,)),
            dma((far, regions)), dma((far, regions)),
            dma((near, regions)), dma((near, regions)),
        ],
        compiler_params=pltpu.CompilerParams(
            collective_id=0, has_side_effects=True, vmem_limit_bytes=48 * 1024 * 1024
        ),
        name="over_batch",
    )(fetched, basis_values, weights)


def shards(basis_values, dens_tiles, region_tiles, point_counts, point_weights):
    owner_count = lax.axis_size("region")
    batch_count = lax.axis_size("batch")
    my_index = lax.axis_index("region")
    region_local = basis_values.shape[0]
    point_local = basis_values.shape[2]
    tile_local = dens_tiles.shape[0]
    requests = 3 * region_local
    owners = region_tiles.reshape(owner_count, requests) // tile_local
    local_ids = region_tiles.reshape(owner_count, requests) % tile_local
    tile_ids = jnp.arange(tile_local, dtype=jnp.int32)
    chosen = (owners == my_index)[:, :, None] & (local_ids[:, :, None] == tile_ids)
    selector = jnp.sum(chosen.astype(jnp.float32), axis=1).astype(jnp.bfloat16)
    my_owners = lax.dynamic_index_in_dim(owners, my_index, 0, keepdims=False)
    outgoing = jnp.einsum(
        "dt,trb->drb", selector, dens_tiles, preferred_element_type=jnp.float32
    ).astype(jnp.bfloat16)
    incoming = lax.all_to_all(outgoing, "region", split_axis=0, concat_axis=0, tiled=True)
    fetched = jnp.take(incoming, my_owners, axis=0)
    live = jnp.arange(point_local, dtype=jnp.int32)[None, :] < point_counts
    weights = jnp.where(live, point_weights, 0.0)[:, :, None]
    pairs = over_batch(fetched, basis_values, weights, batch_count)
    placement = (
        my_owners[:, None] == jnp.arange(owner_count, dtype=jnp.int32)[None, :]
    ).astype(jnp.bfloat16)
    outgoing_sums = jnp.einsum(
        "jd,jrb->drb", placement, pairs, preferred_element_type=jnp.float32
    ).astype(jnp.bfloat16)
    returned = lax.all_to_all(outgoing_sums, "region", split_axis=0, concat_axis=0, tiled=True)
    return jnp.einsum("dt,drb->trb", selector, returned, preferred_element_type=jnp.float32)


def solution(mesh):
    return jax.shard_map(
        shards,
        mesh=mesh,
        in_specs=(
            P("region", None, "batch", None),
            P("region", "batch", None),
            P(),
            P("region", "batch"),
            P("region", "batch"),
        ),
        out_specs=P("region", "batch", None),
        check_vma=False,
    )
```

```python
import functools

import jax
import jax.numpy as jnp
from jax import lax
from jax.experimental import pallas as pl
from jax.experimental.pallas import tpu as pltpu
from jax.sharding import PartitionSpec as P

SLATER = 0.9847450218426964
MESH = pl.DeviceIdType.MESH


def potential(density):
    return -SLATER * density * jnp.exp(jnp.log(density * density + 1.0) * (-1.0 / 3.0))


def batch_kernel(
    ring, far, regions, rows, own_ref, phi_ref, weight_ref, out_ref,
    tiles, pairs, peer, sum_up, got_up, sum_down, got_down,
    up_send, up_recv, down_send, down_recv, side_send, side_recv,
    swap_send, swap_recv, red_up_send, red_up_recv, red_down_send, red_down_recv,
):
    near = ring - 1 - far
    me = lax.axis_index("batch")
    y, c = me // 2, me % 2
    way = 1 - 2 * c
    other = y * 2 + (1 - c)

    def at(k):
        return lax.rem(y + k * way + ring, ring)

    def mine(k):
        return at(k) * 2 + c

    def theirs(k):
        return at(k) * 2 + (1 - c)

    barrier = pltpu.get_barrier_semaphore()
    for target in (mine(1), mine(-1), other):
        pl.semaphore_signal(barrier, inc=1, device_id={"batch": target}, device_id_type=MESH)
    pl.semaphore_wait(barrier, 3)

    def remote(src, dst, send, recv, target):
        return pltpu.make_async_remote_copy(
            src_ref=src, dst_ref=dst, send_sem=send, recv_sem=recv,
            device_id={"batch": target}, device_id_type=MESH,
        )

    def part(r):
        return pl.ds(3 * r, 3)

    def block(r, slot):
        return tiles.at[part(r), slot]

    def up_hop(a, r):
        src = own_ref.at[part(r)] if a == 0 else block(r, mine(-a))
        return remote(src, block(r, mine(-a)), up_send.at[a, r], up_recv.at[a, r], mine(1))

    def up_arrival(a, r):
        slot = block(r, mine(-(a + 1)))
        return remote(slot, slot, up_send.at[a, r], up_recv.at[a, r], mine(1))

    def down_hop(a, r):
        src = own_ref.at[part(r)] if a == 0 else block(r, mine(a))
        return remote(src, block(r, mine(a)), down_send.at[a, r], down_recv.at[a, r], mine(-1))

    def down_arrival(a, r):
        slot = block(r, mine(a + 1))
        return remote(slot, slot, down_send.at[a, r], down_recv.at[a, r], mine(-1))

    def side(i, r):
        if i == 0:
            src, slot = own_ref.at[part(r)], block(r, me)
        else:
            slot = block(r, mine(-i if i <= far else i - far))
            src = slot
        return remote(src, slot, side_send.at[i, r], side_recv.at[i, r], other)

    def side_arrival(i, r):
        k = 0 if i == 0 else (i if i <= far else far - i)
        slot = block(r, theirs(k))
        return remote(slot, slot, side_send.at[i, r], side_recv.at[i, r], other)

    def gather_step(a, r):
        if a == 0:
            up_hop(0, r).start()
            down_hop(0, r).start()
            side(0, r).start()
            tiles[part(r), me] = own_ref[part(r)]
            return
        up_arrival(a - 1, r).wait_recv()
        if a < far:
            up_hop(a, r).start()
        side(a, r).start()
        if a <= near:
            down_arrival(a - 1, r).wait_recv()
            if a < near:
                down_hop(a, r).start()
            side(far + a, r).start()

    def swap(r):
        return remote(
            pairs.at[part(r), :, 1 - c], peer.at[part(r)],
            swap_send.at[r], swap_recv.at[r], other,
        )

    def compute(r):
        for i in range(ring):
            side_arrival(i, r).wait_recv()
        width = phi_ref.shape[-1]
        phi_a, phi_b = phi_ref[r, 0], phi_ref[r, 1]

        def left(values, j):
            matrix = tiles[3 * r + j].reshape(2 * ring * rows, width)
            return jnp.dot(values, matrix, preferred_element_type=jnp.float32)

        wide_a, wide_b = phi_a.astype(jnp.float32), phi_b.astype(jnp.float32)
        density = jnp.sum(
            wide_a * left(phi_a, 0) + wide_b * (2.0 * left(phi_a, 1) + left(phi_b, 2)),
            axis=1, keepdims=True,
        )
        scale = weight_ref[r] * potential(density)
        scaled_a = (scale * wide_a).astype(jnp.bfloat16)
        scaled_b = (scale * wide_b).astype(jnp.bfloat16)
        for j, (lhs, rhs) in enumerate(((phi_a, scaled_a), (phi_a, scaled_b), (phi_b, scaled_b))):
            product = lax.dot_general(
                lhs, rhs, (((0,), (0,)), ((), ())), preferred_element_type=jnp.float32
            )
            pairs[3 * r + j] = product.astype(jnp.bfloat16).reshape(ring, 2, rows, width)
        swap(r).start()

    def chip_sum(r, k):
        return pairs[part(r), at(k), c].astype(jnp.float32) + peer[part(r), at(k)].astype(jnp.float32)

    def red_up(s, r):
        return remote(
            sum_up.at[s, part(r)], got_up.at[s, part(r)],
            red_up_send.at[s, r], red_up_recv.at[s, r], mine(1),
        )

    def red_down(s, r):
        return remote(
            sum_down.at[s, part(r)], got_down.at[s, part(r)],
            red_down_send.at[s, r], red_down_recv.at[s, r], mine(-1),
        )

    def reduce_step(s, r):
        if s == 0:
            swap(r).wait_recv()
        total = chip_sum(r, far - s)
        if s > 0:
            red_up(s - 1, r).wait_recv()
            total = total + got_up[s - 1, part(r)].astype(jnp.float32)
        sum_up[s, part(r)] = total.astype(jnp.bfloat16)
        red_up(s, r).start()
        if s < near:
            total = chip_sum(r, s - near)
            if s > 0:
                red_down(s - 1, r).wait_recv()
                total = total + got_down[s - 1, part(r)].astype(jnp.float32)
            sum_down[s, part(r)] = total.astype(jnp.bfloat16)
            red_down(s, r).start()

    def finish(r):
        red_up(far - 1, r).wait_recv()
        red_down(near - 1, r).wait_recv()
        total = chip_sum(r, 0)
        total = total + got_up[far - 1, part(r)].astype(jnp.float32)
        total = total + got_down[near - 1, part(r)].astype(jnp.float32)
        out_ref[part(r)] = total.astype(out_ref.dtype)

    last = 2 * far + 2
    for r in range(regions):
        gather_step(0, r)
    for t in range(1, last + regions):
        for r in range(regions):
            stage = t - r
            if 1 <= stage <= far:
                gather_step(stage, r)
            elif far + 2 <= stage < last:
                reduce_step(stage - far - 2, r)
            elif stage == last:
                finish(r)
        if 0 <= t - far - 1 < regions:
            compute(t - far - 1)

    for r in range(regions):
        for a in range(far):
            up_hop(a, r).wait_send()
            red_up(a, r).wait_send()
        for a in range(near):
            down_hop(a, r).wait_send()
            red_down(a, r).wait_send()
        for i in range(ring):
            side(i, r).wait_send()
        swap(r).wait_send()


def over_batch(fetched, basis_values, weights, batch_count):
    ring = batch_count // 2
    far = ring // 2
    near = ring - 1 - far
    regions = basis_values.shape[0]
    requests, rows, width = fetched.shape
    dma = pltpu.SemaphoreType.DMA
    half = jnp.bfloat16
    vmem = pl.BlockSpec(memory_space=pltpu.VMEM)
    return pl.pallas_call(
        functools.partial(batch_kernel, ring, far, regions, rows),
        out_shape=jax.ShapeDtypeStruct((requests, rows, width), half),
        in_specs=[vmem] * 3,
        out_specs=vmem,
        scratch_shapes=[
            pltpu.VMEM((requests, batch_count, rows, width), half),
            pltpu.VMEM((requests, ring, 2, rows, width), half),
            pltpu.VMEM((requests, ring, rows, width), half),
            pltpu.VMEM((far, requests, rows, width), half),
            pltpu.VMEM((far, requests, rows, width), half),
            pltpu.VMEM((near, requests, rows, width), half),
            pltpu.VMEM((near, requests, rows, width), half),
            dma((far, regions)), dma((far, regions)),
            dma((near, regions)), dma((near, regions)),
            dma((ring, regions)), dma((ring, regions)),
            dma((regions,)), dma((regions,)),
            dma((far, regions)), dma((far, regions)),
            dma((near, regions)), dma((near, regions)),
        ],
        compiler_params=pltpu.CompilerParams(
            collective_id=0, has_side_effects=True, vmem_limit_bytes=48 * 1024 * 1024
        ),
        name="over_batch",
    )(fetched, basis_values, weights)


def plane(columns, ring):
    m = lax.axis_index("region")
    x, z = m // ring, m % ring
    way = 1 - 2 * (lax.axis_index("batch") % 2)

    def at(k):
        return lax.rem(z + k * way + ring, ring)

    def along_z(k):
        return x * ring + at(k)

    def along_x(d):
        return lax.rem(x + d, columns) * ring + z

    def greet():
        barrier = pltpu.get_barrier_semaphore()
        targets = [along_z(1), along_z(-1)] + [along_x(d) for d in range(1, columns)]
        for target in targets:
            pl.semaphore_signal(barrier, inc=1, device_id={"region": target}, device_id_type=MESH)
        pl.semaphore_wait(barrier, len(targets))

    return m, x, z, at, along_z, along_x, greet


def to_region(src, dst, send, recv, target):
    return pltpu.make_async_remote_copy(
        src_ref=src, dst_ref=dst, send_sem=send, recv_sem=recv,
        device_id={"region": target}, device_id_type=MESH,
    )


def fetch_kernel(columns, ring, far, table_ref, owner_ref, own_ref, out_ref, stage, landed,
                 up_send, up_recv, down_send, down_recv, x_send, x_recv, *held):
    near = ring - 1 - far
    kept = own_ref.shape[0]
    m, x, z, at, along_z, along_x, greet = plane(columns, ring)
    greet()

    def source(i):
        return own_ref if i == 0 else held[i - 1]

    def place(i):
        return 0 if i == 0 else (-i if i <= far else i - far)

    def up(a, t):
        return to_region(source(a).at[t], held[a].at[t], up_send.at[a, t], up_recv.at[a, t], along_z(1))

    def down(a, t):
        src = own_ref if a == 0 else held[far + a - 1]
        return to_region(
            src.at[t], held[far + a].at[t], down_send.at[a, t], down_recv.at[a, t], along_z(-1)
        )

    def across(d, i):
        return to_region(
            stage.at[d - 1, i], landed.at[along_z(place(i))],
            x_send.at[d - 1, i], x_recv.at[d - 1, i], along_x(d),
        )

    def arrival(d, i):
        slot = landed.at[lax.rem(x + columns - d, columns) * ring + at(place(i))]
        return to_region(slot, slot, x_send.at[d - 1, i], x_recv.at[d - 1, i], along_x(d))

    def pass_on(i):
        zo = at(place(i))
        for d in range(1, columns):
            wanted = jnp.maximum(table_ref[lax.rem(x + d, columns), zo], 0)
            stage[d - 1, i] = source(i)[wanted]
            across(d, i).start()
        landed[along_z(place(i))] = source(i)[jnp.maximum(table_ref[x, zo], 0)]

    for t in range(kept):
        up(0, t).start()
        down(0, t).start()
    pass_on(0)
    for a in range(1, far + 1):
        for t in range(kept):
            up(a - 1, t).wait_recv()
            if a < far:
                up(a, t).start()
            if a <= near:
                down(a - 1, t).wait_recv()
                if a < near:
                    down(a, t).start()
        pass_on(a)
        if a <= near:
            pass_on(far + a)
    for i in range(ring):
        for d in range(1, columns):
            arrival(d, i).wait_recv()
    for j in range(out_ref.shape[0]):
        out_ref[j] = landed[owner_ref[j]]
    for t in range(kept):
        for a in range(far):
            up(a, t).wait_send()
        for a in range(near):
            down(a, t).wait_send()
    for i in range(ring):
        for d in range(1, columns):
            across(d, i).wait_send()


def give_kernel(columns, ring, far, table_ref, request_ref, pairs_ref, out_ref, stage, landed,
                sum_up, got_up, sum_down, got_down,
                up_send, up_recv, down_send, down_recv, x_send, x_recv):
    near = ring - 1 - far
    kept = out_ref.shape[0]
    m, x, z, at, along_z, along_x, greet = plane(columns, ring)
    greet()

    def across(d, i):
        return to_region(
            stage.at[d - 1, i], landed.at[d - 1, i], x_send.at[d - 1, i], x_recv.at[d - 1, i], along_x(d)
        )

    def up(s, t):
        return to_region(sum_up.at[s, t], got_up.at[s, t], up_send.at[s, t], up_recv.at[s, t], along_z(1))

    def down(s, t):
        return to_region(
            sum_down.at[s, t], got_down.at[s, t], down_send.at[s, t], down_recv.at[s, t], along_z(-1)
        )

    order = []
    for s in range(far):
        order.append(far - s)
        if s < near:
            order.append(s - near)
    order.append(0)
    for k in order:
        for d in range(1, columns):
            request = request_ref[lax.rem(x + d, columns), at(k)]
            stage[d - 1, k % ring] = pairs_ref[request]
            across(d, k % ring).start()

    def placed(k):
        for d in range(1, columns):
            across(d, k % ring).wait_recv()
        terms = [(table_ref[x, at(k)], pairs_ref[request_ref[x, at(k)]].astype(jnp.float32))]
        for d in range(1, columns):
            sender = lax.rem(x + columns - d, columns)
            terms.append((table_ref[sender, at(k)], landed[d - 1, k % ring].astype(jnp.float32)))

        def tile(t):
            total = jnp.zeros(pairs_ref.shape[1:], jnp.float32)
            for wanted, values in terms:
                total = total + jnp.where(jnp.full(values.shape, wanted, jnp.int32) == t, values, 0.0)
            return total

        return tile

    for s in range(far):
        tile = placed(far - s)
        for t in range(kept):
            total = tile(t)
            if s > 0:
                up(s - 1, t).wait_recv()
                total = total + got_up[s - 1, t].astype(jnp.float32)
            sum_up[s, t] = total.astype(sum_up.dtype)
            up(s, t).start()
        if s < near:
            tile = placed(s - near)
            for t in range(kept):
                total = tile(t)
                if s > 0:
                    down(s - 1, t).wait_recv()
                    total = total + got_down[s - 1, t].astype(jnp.float32)
                sum_down[s, t] = total.astype(sum_down.dtype)
                down(s, t).start()
    tile = placed(0)
    for t in range(kept):
        total = tile(t)
        down(near - 1, t).wait_recv()
        total = total + got_down[near - 1, t].astype(jnp.float32)
        up(far - 1, t).wait_recv()
        out_ref[t] = total + got_up[far - 1, t].astype(jnp.float32)
    for t in range(kept):
        for s in range(far):
            up(s, t).wait_send()
        for s in range(near):
            down(s, t).wait_send()
    for k in order:
        for d in range(1, columns):
            across(d, k % ring).wait_send()


def over_region(kernel, name, collective_id, scratch, out, columns, ring, far, table, index, values):
    vmem, smem = pl.BlockSpec(memory_space=pltpu.VMEM), pl.BlockSpec(memory_space=pltpu.SMEM)
    return pl.pallas_call(
        functools.partial(kernel, columns, ring, far),
        out_shape=out,
        in_specs=[smem, smem, vmem],
        out_specs=vmem,
        scratch_shapes=scratch,
        compiler_params=pltpu.CompilerParams(
            collective_id=collective_id, has_side_effects=True, vmem_limit_bytes=32 * 1024 * 1024
        ),
        name=name,
    )(table, index, values)


COLUMNS = 4


def plane_semaphores(columns, ring, far, kept):
    dma = pltpu.SemaphoreType.DMA
    near = ring - 1 - far
    return [
        dma((far, kept)), dma((far, kept)), dma((near, kept)), dma((near, kept)),
        dma((columns - 1, ring)), dma((columns - 1, ring)),
    ]


def fetch(table, my_owners, dens_tiles, ring):
    far = ring // 2
    kept, rows, width = dens_tiles.shape
    kind = dens_tiles.dtype
    scratch = [
        pltpu.VMEM((COLUMNS - 1, ring, rows, width), kind),
        pltpu.VMEM((COLUMNS * ring, rows, width), kind),
    ]
    scratch += plane_semaphores(COLUMNS, ring, far, kept)
    scratch += [pltpu.VMEM((kept, rows, width), kind)] * (ring - 1)
    out = jax.ShapeDtypeStruct((my_owners.shape[0], rows, width), kind)
    return over_region(
        fetch_kernel, "fetch", 1, scratch, out, COLUMNS, ring, far, table, my_owners, dens_tiles
    )


def give(table, request, pairs, kept, ring):
    far = ring // 2
    near = ring - 1 - far
    rows, width = pairs.shape[1:]
    kind = pairs.dtype
    scratch = [pltpu.VMEM((COLUMNS - 1, ring, rows, width), kind)] * 2
    scratch += [pltpu.VMEM((far, kept, rows, width), kind)] * 2
    scratch += [pltpu.VMEM((near, kept, rows, width), kind)] * 2
    scratch += plane_semaphores(COLUMNS, ring, far, kept)
    out = jax.ShapeDtypeStruct((kept, rows, width), jnp.float32)
    return over_region(
        give_kernel, "give", 2, scratch, out, COLUMNS, ring, far, table, request, pairs
    )


def shards(basis_values, dens_tiles, region_tiles, point_counts, point_weights):
    owner_count = lax.axis_size("region")
    batch_count = lax.axis_size("batch")
    ring = owner_count // COLUMNS
    my_index = lax.axis_index("region")
    region_local = basis_values.shape[0]
    point_local = basis_values.shape[2]
    tile_local = dens_tiles.shape[0]
    requests = 3 * region_local
    owners = region_tiles.reshape(owner_count, requests) // tile_local
    local_ids = region_tiles.reshape(owner_count, requests) % tile_local
    mine = owners[:, :, None] == jnp.arange(owner_count, dtype=jnp.int32)
    wanted = jnp.sum(jnp.where(mine, local_ids[:, :, None] + 1, 0), axis=1) - 1
    order = jnp.arange(requests, dtype=jnp.int32)
    request_of = jnp.sum(jnp.where(mine, order[None, :, None], 0), axis=1)
    my_owners = lax.dynamic_index_in_dim(owners, my_index, 0, keepdims=False)
    request = lax.dynamic_index_in_dim(request_of, my_index, 0, keepdims=False)
    request = request.reshape(COLUMNS, ring)
    table = wanted.reshape(COLUMNS, ring, COLUMNS, ring)
    table = lax.dynamic_index_in_dim(table, my_index % ring, 1, keepdims=False)
    table = lax.dynamic_index_in_dim(table, my_index // ring, 1, keepdims=False)
    fetched = fetch(table, my_owners, dens_tiles, ring)
    live = jnp.arange(point_local, dtype=jnp.int32)[None, :] < point_counts
    weights = jnp.where(live, point_weights, 0.0)[:, :, None]
    pairs = over_batch(fetched, basis_values, weights, batch_count)
    return give(table, request, pairs, tile_local, ring)


def solution(mesh):
    return jax.shard_map(
        shards,
        mesh=mesh,
        in_specs=(
            P("region", None, "batch", None),
            P("region", "batch", None),
            P(),
            P("region", "batch"),
            P("region", "batch"),
        ),
        out_specs=P("region", "batch", None),
        check_vma=False,
    )
```

```python
import functools

import jax
import jax.numpy as jnp
from jax import lax
from jax.experimental import pallas as pl
from jax.experimental.pallas import tpu as pltpu
from jax.sharding import PartitionSpec as P

SLATER = 0.9847450218426964
MESH = pl.DeviceIdType.MESH


def potential(density):
    return -SLATER * density * jnp.exp(jnp.log(density * density + 1.0) * (-1.0 / 3.0))


GATHER, COMPUTE, REDUCE, FINISH = range(4)


def schedule(far, near, regions):
    if (far, regions) != (4, 4):
        order = [(GATHER, a, r) for a in range(far + 1) for r in range(regions)]
        order += [(COMPUTE, r) for r in range(regions)]
        order += [(REDUCE, s, r) for s in range(far) for r in range(regions)]
        return order + [(FINISH, r) for r in range(regions)]
    order = []
    for t in range(5):
        order += [(GATHER, t, 0), (GATHER, t, 1)]
        if t >= 2:
            order += [(GATHER, t - 2, 2), (GATHER, t - 2, 3)]
    order += [(COMPUTE, 0), (GATHER, 3, 2), (GATHER, 3, 3), (COMPUTE, 1), (REDUCE, 0, 0)]
    order += [(GATHER, 4, 2), (REDUCE, 0, 1), (GATHER, 4, 3), (REDUCE, 1, 0), (COMPUTE, 2)]
    order += [(REDUCE, 1, 1), (REDUCE, 2, 0), (REDUCE, 0, 2), (COMPUTE, 3), (REDUCE, 1, 2)]
    order += [(REDUCE, 2, 1), (REDUCE, 3, 0), (REDUCE, 0, 3), (REDUCE, 2, 2), (REDUCE, 3, 1)]
    order += [(REDUCE, 1, 3), (FINISH, 0), (REDUCE, 3, 2), (REDUCE, 2, 3), (FINISH, 1)]
    return order + [(REDUCE, 3, 3), (FINISH, 2), (FINISH, 3)]


def batch_kernel(
    ring, far, regions, rows, own_ref, basis_ref, weight_ref, out_ref,
    phi_ref, load, tiles, pairs, peer, sum_up, got_up, sum_down, got_down,
    up_send, up_recv, down_send, down_recv, side_send, side_recv,
    swap_send, swap_recv, red_up_send, red_up_recv, red_down_send, red_down_recv,
):
    near = ring - 1 - far
    me = lax.axis_index("batch")
    y, c = me // 2, me % 2
    way = 1 - 2 * c
    other = y * 2 + (1 - c)

    def at(k):
        return lax.rem(y + k * way + ring, ring)

    def mine(k):
        return at(k) * 2 + c

    def theirs(k):
        return at(k) * 2 + (1 - c)

    def values(r):
        return pltpu.make_async_copy(basis_ref.at[r], phi_ref.at[r], load.at[r])

    for r in range(regions):
        values(r).start()
    barrier = pltpu.get_barrier_semaphore()
    for target in (mine(1), mine(-1), other):
        pl.semaphore_signal(barrier, inc=1, device_id={"batch": target}, device_id_type=MESH)
    pl.semaphore_wait(barrier, 3)

    def remote(src, dst, send, recv, target):
        return pltpu.make_async_remote_copy(
            src_ref=src, dst_ref=dst, send_sem=send, recv_sem=recv,
            device_id={"batch": target}, device_id_type=MESH,
        )

    def part(r):
        return pl.ds(3 * r, 3)

    def block(r, slot):
        return tiles.at[part(r), slot]

    def up_hop(a, r):
        src = own_ref.at[part(r)] if a == 0 else block(r, mine(-a))
        return remote(src, block(r, mine(-a)), up_send.at[a, r], up_recv.at[a, r], mine(1))

    def up_arrival(a, r):
        slot = block(r, mine(-(a + 1)))
        return remote(slot, slot, up_send.at[a, r], up_recv.at[a, r], mine(1))

    def down_hop(a, r):
        src = own_ref.at[part(r)] if a == 0 else block(r, mine(a))
        return remote(src, block(r, mine(a)), down_send.at[a, r], down_recv.at[a, r], mine(-1))

    def down_arrival(a, r):
        slot = block(r, mine(a + 1))
        return remote(slot, slot, down_send.at[a, r], down_recv.at[a, r], mine(-1))

    def side(i, r):
        if i == 0:
            src, slot = own_ref.at[part(r)], block(r, me)
        else:
            slot = block(r, mine(-i if i <= far else i - far))
            src = slot
        return remote(src, slot, side_send.at[i, r], side_recv.at[i, r], other)

    def side_arrival(i, r):
        k = 0 if i == 0 else (i if i <= far else far - i)
        slot = block(r, theirs(k))
        return remote(slot, slot, side_send.at[i, r], side_recv.at[i, r], other)

    def gather_step(a, r):
        if a == 0:
            up_hop(0, r).start()
            down_hop(0, r).start()
            side(0, r).start()
            tiles[part(r), me] = own_ref[part(r)]
            return
        up_arrival(a - 1, r).wait_recv()
        if a < far:
            up_hop(a, r).start()
        side(a, r).start()
        if a <= near:
            down_arrival(a - 1, r).wait_recv()
            if a < near:
                down_hop(a, r).start()
            side(far + a, r).start()

    def swap(r):
        return remote(
            pairs.at[part(r), :, 1 - c], peer.at[part(r)],
            swap_send.at[r], swap_recv.at[r], other,
        )

    def compute(r):
        for i in range(ring):
            side_arrival(i, r).wait_recv()
        values(r).wait()
        width = phi_ref.shape[-1]
        phi_a, phi_b = phi_ref[r, 0], phi_ref[r, 1]

        def left(phi, j):
            matrix = tiles[3 * r + j].reshape(2 * ring * rows, width)
            return jnp.dot(phi, matrix, preferred_element_type=jnp.float32)

        wide_a, wide_b = phi_a.astype(jnp.float32), phi_b.astype(jnp.float32)
        density = jnp.sum(
            wide_a * left(phi_a, 0) + wide_b * (2.0 * left(phi_a, 1) + left(phi_b, 2)),
            axis=1, keepdims=True,
        )
        scale = weight_ref[r] * potential(density)
        scaled_a = (scale * wide_a).astype(jnp.bfloat16)
        scaled_b = (scale * wide_b).astype(jnp.bfloat16)
        for j, (lhs, rhs) in enumerate(((phi_a, scaled_a), (phi_a, scaled_b), (phi_b, scaled_b))):
            product = lax.dot_general(
                lhs, rhs, (((0,), (0,)), ((), ())), preferred_element_type=jnp.float32
            )
            pairs[3 * r + j] = product.astype(jnp.bfloat16).reshape(ring, 2, rows, width)
        swap(r).start()

    def chip_sum(r, k):
        return pairs[part(r), at(k), c].astype(jnp.float32) + peer[part(r), at(k)].astype(jnp.float32)

    def red_up(s, r):
        return remote(
            sum_up.at[s, part(r)], got_up.at[s, part(r)],
            red_up_send.at[s, r], red_up_recv.at[s, r], mine(1),
        )

    def red_down(s, r):
        return remote(
            sum_down.at[s, part(r)], got_down.at[s, part(r)],
            red_down_send.at[s, r], red_down_recv.at[s, r], mine(-1),
        )

    def reduce_step(s, r):
        if s == 0:
            swap(r).wait_recv()
        total = chip_sum(r, far - s)
        if s > 0:
            red_up(s - 1, r).wait_recv()
            total = total + got_up[s - 1, part(r)].astype(jnp.float32)
        sum_up[s, part(r)] = total.astype(jnp.bfloat16)
        red_up(s, r).start()
        if s < near:
            total = chip_sum(r, s - near)
            if s > 0:
                red_down(s - 1, r).wait_recv()
                total = total + got_down[s - 1, part(r)].astype(jnp.float32)
            sum_down[s, part(r)] = total.astype(jnp.bfloat16)
            red_down(s, r).start()

    def finish(r):
        red_up(far - 1, r).wait_recv()
        red_down(near - 1, r).wait_recv()
        total = chip_sum(r, 0)
        total = total + got_up[far - 1, part(r)].astype(jnp.float32)
        total = total + got_down[near - 1, part(r)].astype(jnp.float32)
        out_ref[part(r)] = total.astype(out_ref.dtype)

    for action, *where in schedule(far, near, regions):
        (gather_step, compute, reduce_step, finish)[action](*where)

    for r in range(regions):
        for a in range(far):
            up_hop(a, r).wait_send()
            red_up(a, r).wait_send()
        for a in range(near):
            down_hop(a, r).wait_send()
            red_down(a, r).wait_send()
        for i in range(ring):
            side(i, r).wait_send()
        swap(r).wait_send()


def over_batch(fetched, basis_values, weights, batch_count):
    ring = batch_count // 2
    far = ring // 2
    near = ring - 1 - far
    regions = basis_values.shape[0]
    requests, rows, width = fetched.shape
    dma = pltpu.SemaphoreType.DMA
    half = jnp.bfloat16
    vmem = pl.BlockSpec(memory_space=pltpu.VMEM)
    return pl.pallas_call(
        functools.partial(batch_kernel, ring, far, regions, rows),
        out_shape=jax.ShapeDtypeStruct((requests, rows, width), half),
        in_specs=[vmem, pl.BlockSpec(memory_space=pltpu.HBM), vmem],
        out_specs=vmem,
        scratch_shapes=[
            pltpu.VMEM(basis_values.shape, half), dma((regions,)),
            pltpu.VMEM((requests, batch_count, rows, width), half),
            pltpu.VMEM((requests, ring, 2, rows, width), half),
            pltpu.VMEM((requests, ring, rows, width), half),
            pltpu.VMEM((far, requests, rows, width), half),
            pltpu.VMEM((far, requests, rows, width), half),
            pltpu.VMEM((near, requests, rows, width), half),
            pltpu.VMEM((near, requests, rows, width), half),
            dma((far, regions)), dma((far, regions)),
            dma((near, regions)), dma((near, regions)),
            dma((ring, regions)), dma((ring, regions)),
            dma((regions,)), dma((regions,)),
            dma((far, regions)), dma((far, regions)),
            dma((near, regions)), dma((near, regions)),
        ],
        compiler_params=pltpu.CompilerParams(
            collective_id=0, has_side_effects=True, vmem_limit_bytes=48 * 1024 * 1024
        ),
        name="over_batch",
    )(fetched, basis_values, weights)


def plane(columns, ring):
    m = lax.axis_index("region")
    x, z = m // ring, m % ring
    way = 1 - 2 * (lax.axis_index("batch") % 2)

    def at(k):
        return lax.rem(z + k * way + ring, ring)

    def along_z(k):
        return x * ring + at(k)

    def along_x(d):
        return lax.rem(x + d, columns) * ring + z

    def greet():
        barrier = pltpu.get_barrier_semaphore()
        targets = [along_z(1), along_z(-1)] + [along_x(d) for d in range(1, columns)]
        for target in targets:
            pl.semaphore_signal(barrier, inc=1, device_id={"region": target}, device_id_type=MESH)
        pl.semaphore_wait(barrier, len(targets))

    return m, x, z, at, along_z, along_x, greet


def to_region(src, dst, send, recv, target):
    return pltpu.make_async_remote_copy(
        src_ref=src, dst_ref=dst, send_sem=send, recv_sem=recv,
        device_id={"region": target}, device_id_type=MESH,
    )


def fetch_kernel(columns, ring, far, table_ref, owner_ref, own_ref, out_ref, stage, landed,
                 up_send, up_recv, down_send, down_recv, x_send, x_recv, *held):
    near = ring - 1 - far
    kept = own_ref.shape[0]
    m, x, z, at, along_z, along_x, greet = plane(columns, ring)
    greet()

    def source(i):
        return own_ref if i == 0 else held[i - 1]

    def place(i):
        return 0 if i == 0 else (-i if i <= far else i - far)

    def up(a, t):
        return to_region(source(a).at[t], held[a].at[t], up_send.at[a, t], up_recv.at[a, t], along_z(1))

    def down(a, t):
        src = own_ref if a == 0 else held[far + a - 1]
        return to_region(
            src.at[t], held[far + a].at[t], down_send.at[a, t], down_recv.at[a, t], along_z(-1)
        )

    def across(d, i):
        return to_region(
            stage.at[d - 1, i], landed.at[along_z(place(i))],
            x_send.at[d - 1, i], x_recv.at[d - 1, i], along_x(d),
        )

    def arrival(d, i):
        slot = landed.at[lax.rem(x + columns - d, columns) * ring + at(place(i))]
        return to_region(slot, slot, x_send.at[d - 1, i], x_recv.at[d - 1, i], along_x(d))

    def pass_on(i):
        zo = at(place(i))
        for d in range(1, columns):
            wanted = jnp.maximum(table_ref[lax.rem(x + d, columns), zo], 0)
            stage[d - 1, i] = source(i)[wanted]
            across(d, i).start()
        landed[along_z(place(i))] = source(i)[jnp.maximum(table_ref[x, zo], 0)]

    for t in range(kept):
        up(0, t).start()
        down(0, t).start()
    pass_on(0)
    for a in range(1, far + 1):
        for t in range(kept):
            up(a - 1, t).wait_recv()
            if a < far:
                up(a, t).start()
            if a <= near:
                down(a - 1, t).wait_recv()
                if a < near:
                    down(a, t).start()
        pass_on(a)
        if a <= near:
            pass_on(far + a)
    for i in range(ring):
        for d in range(1, columns):
            arrival(d, i).wait_recv()
    for j in range(out_ref.shape[0]):
        out_ref[j] = landed[owner_ref[j]]
    for t in range(kept):
        for a in range(far):
            up(a, t).wait_send()
        for a in range(near):
            down(a, t).wait_send()
    for i in range(ring):
        for d in range(1, columns):
            across(d, i).wait_send()


def give_kernel(columns, ring, far, table_ref, request_ref, pairs_ref, out_ref, stage, landed,
                sum_up, got_up, sum_down, got_down,
                up_send, up_recv, down_send, down_recv, x_send, x_recv):
    near = ring - 1 - far
    kept = out_ref.shape[0]
    m, x, z, at, along_z, along_x, greet = plane(columns, ring)
    greet()

    def across(d, i):
        return to_region(
            stage.at[d - 1, i], landed.at[d - 1, i], x_send.at[d - 1, i], x_recv.at[d - 1, i], along_x(d)
        )

    def up(s, t):
        return to_region(sum_up.at[s, t], got_up.at[s, t], up_send.at[s, t], up_recv.at[s, t], along_z(1))

    def down(s, t):
        return to_region(
            sum_down.at[s, t], got_down.at[s, t], down_send.at[s, t], down_recv.at[s, t], along_z(-1)
        )

    order = []
    for s in range(far):
        order.append(far - s)
        if s < near:
            order.append(s - near)
    order.append(0)
    for k in order:
        for d in range(1, columns):
            request = request_ref[lax.rem(x + d, columns), at(k)]
            stage[d - 1, k % ring] = pairs_ref[request]
            across(d, k % ring).start()

    def placed(k):
        for d in range(1, columns):
            across(d, k % ring).wait_recv()
        terms = [(table_ref[x, at(k)], pairs_ref[request_ref[x, at(k)]].astype(jnp.float32))]
        for d in range(1, columns):
            sender = lax.rem(x + columns - d, columns)
            terms.append((table_ref[sender, at(k)], landed[d - 1, k % ring].astype(jnp.float32)))

        def tile(t):
            total = jnp.zeros(pairs_ref.shape[1:], jnp.float32)
            for wanted, values in terms:
                total = total + jnp.where(jnp.full(values.shape, wanted, jnp.int32) == t, values, 0.0)
            return total

        return tile

    for s in range(far):
        tile = placed(far - s)
        for t in range(kept):
            total = tile(t)
            if s > 0:
                up(s - 1, t).wait_recv()
                total = total + got_up[s - 1, t].astype(jnp.float32)
            sum_up[s, t] = total.astype(sum_up.dtype)
            up(s, t).start()
        if s < near:
            tile = placed(s - near)
            for t in range(kept):
                total = tile(t)
                if s > 0:
                    down(s - 1, t).wait_recv()
                    total = total + got_down[s - 1, t].astype(jnp.float32)
                sum_down[s, t] = total.astype(sum_down.dtype)
                down(s, t).start()
    tile = placed(0)
    for t in range(kept):
        total = tile(t)
        down(near - 1, t).wait_recv()
        total = total + got_down[near - 1, t].astype(jnp.float32)
        up(far - 1, t).wait_recv()
        out_ref[t] = total + got_up[far - 1, t].astype(jnp.float32)
    for t in range(kept):
        for s in range(far):
            up(s, t).wait_send()
        for s in range(near):
            down(s, t).wait_send()
    for k in order:
        for d in range(1, columns):
            across(d, k % ring).wait_send()


def over_region(kernel, name, collective_id, scratch, out, columns, ring, far, table, index, values):
    vmem, smem = pl.BlockSpec(memory_space=pltpu.VMEM), pl.BlockSpec(memory_space=pltpu.SMEM)
    return pl.pallas_call(
        functools.partial(kernel, columns, ring, far),
        out_shape=out,
        in_specs=[smem, smem, vmem],
        out_specs=vmem,
        scratch_shapes=scratch,
        compiler_params=pltpu.CompilerParams(
            collective_id=collective_id, has_side_effects=True, vmem_limit_bytes=32 * 1024 * 1024
        ),
        name=name,
    )(table, index, values)


COLUMNS = 4


def plane_semaphores(columns, ring, far, kept):
    dma = pltpu.SemaphoreType.DMA
    near = ring - 1 - far
    return [
        dma((far, kept)), dma((far, kept)), dma((near, kept)), dma((near, kept)),
        dma((columns - 1, ring)), dma((columns - 1, ring)),
    ]


def fetch(table, my_owners, dens_tiles, ring):
    far = ring // 2
    kept, rows, width = dens_tiles.shape
    kind = dens_tiles.dtype
    scratch = [
        pltpu.VMEM((COLUMNS - 1, ring, rows, width), kind),
        pltpu.VMEM((COLUMNS * ring, rows, width), kind),
    ]
    scratch += plane_semaphores(COLUMNS, ring, far, kept)
    scratch += [pltpu.VMEM((kept, rows, width), kind)] * (ring - 1)
    out = jax.ShapeDtypeStruct((my_owners.shape[0], rows, width), kind)
    return over_region(
        fetch_kernel, "fetch", 1, scratch, out, COLUMNS, ring, far, table, my_owners, dens_tiles
    )


def give(table, request, pairs, kept, ring):
    far = ring // 2
    near = ring - 1 - far
    rows, width = pairs.shape[1:]
    kind = pairs.dtype
    scratch = [pltpu.VMEM((COLUMNS - 1, ring, rows, width), kind)] * 2
    scratch += [pltpu.VMEM((far, kept, rows, width), kind)] * 2
    scratch += [pltpu.VMEM((near, kept, rows, width), kind)] * 2
    scratch += plane_semaphores(COLUMNS, ring, far, kept)
    out = jax.ShapeDtypeStruct((kept, rows, width), jnp.float32)
    return over_region(
        give_kernel, "give", 2, scratch, out, COLUMNS, ring, far, table, request, pairs
    )


def shards(basis_values, dens_tiles, region_tiles, point_counts, point_weights):
    owner_count = lax.axis_size("region")
    batch_count = lax.axis_size("batch")
    ring = owner_count // COLUMNS
    my_index = lax.axis_index("region")
    region_local = basis_values.shape[0]
    point_local = basis_values.shape[2]
    tile_local = dens_tiles.shape[0]
    requests = 3 * region_local
    owners = region_tiles.reshape(owner_count, requests) // tile_local
    local_ids = region_tiles.reshape(owner_count, requests) % tile_local
    mine = owners[:, :, None] == jnp.arange(owner_count, dtype=jnp.int32)
    wanted = jnp.sum(jnp.where(mine, local_ids[:, :, None] + 1, 0), axis=1) - 1
    order = jnp.arange(requests, dtype=jnp.int32)
    request_of = jnp.sum(jnp.where(mine, order[None, :, None], 0), axis=1)
    my_owners = lax.dynamic_index_in_dim(owners, my_index, 0, keepdims=False)
    request = lax.dynamic_index_in_dim(request_of, my_index, 0, keepdims=False)
    request = request.reshape(COLUMNS, ring)
    table = wanted.reshape(COLUMNS, ring, COLUMNS, ring)
    table = lax.dynamic_index_in_dim(table, my_index % ring, 1, keepdims=False)
    table = lax.dynamic_index_in_dim(table, my_index // ring, 1, keepdims=False)
    fetched = fetch(table, my_owners, dens_tiles, ring)
    live = jnp.arange(point_local, dtype=jnp.int32)[None, :] < point_counts
    weights = jnp.where(live, point_weights, 0.0)[:, :, None]
    pairs = over_batch(fetched, basis_values, weights, batch_count)
    return give(table, request, pairs, tile_local, ring)


def solution(mesh):
    return jax.shard_map(
        shards,
        mesh=mesh,
        in_specs=(
            P("region", None, "batch", None),
            P("region", "batch", None),
            P(),
            P("region", "batch"),
            P("region", "batch"),
        ),
        out_specs=P("region", "batch", None),
        check_vma=False,
    )
```

```python
import functools

import jax
import jax.numpy as jnp
from jax import lax
from jax.experimental import pallas as pl
from jax.experimental.pallas import tpu as pltpu
from jax.sharding import PartitionSpec as P

SLATER = 0.9847450218426964
MESH = pl.DeviceIdType.MESH


def potential(density):
    return -SLATER * density * jnp.exp(jnp.log(density * density + 1.0) * (-1.0 / 3.0))


GATHER, COMPUTE, REDUCE, FINISH = range(4)


def schedule(far, near, regions):
    if (far, regions) != (4, 4):
        order = [(GATHER, a, r) for a in range(far + 1) for r in range(regions)]
        order += [(COMPUTE, r) for r in range(regions)]
        order += [(REDUCE, s, r) for s in range(far) for r in range(regions)]
        return order + [(FINISH, r) for r in range(regions)]
    order = []
    for t in range(5):
        order += [(GATHER, t, 0), (GATHER, t, 1)]
        if t >= 2:
            order += [(GATHER, t - 2, 2), (GATHER, t - 2, 3)]
    order += [(COMPUTE, 0), (GATHER, 3, 2), (GATHER, 3, 3), (COMPUTE, 1), (REDUCE, 0, 0)]
    order += [(GATHER, 4, 2), (REDUCE, 0, 1), (GATHER, 4, 3), (REDUCE, 1, 0), (COMPUTE, 2)]
    order += [(REDUCE, 1, 1), (REDUCE, 2, 0), (REDUCE, 0, 2), (COMPUTE, 3), (REDUCE, 1, 2)]
    order += [(REDUCE, 2, 1), (REDUCE, 3, 0), (REDUCE, 0, 3), (REDUCE, 2, 2), (REDUCE, 3, 1)]
    order += [(REDUCE, 1, 3), (FINISH, 0), (REDUCE, 3, 2), (REDUCE, 2, 3), (FINISH, 1)]
    return order + [(REDUCE, 3, 3), (FINISH, 2), (FINISH, 3)]


def batch_kernel(
    ring, far, regions, rows, own_ref, basis_ref, weight_ref, out_ref,
    phi_ref, load, tiles, pairs, peer, sum_up, got_up, sum_down, got_down,
    up_send, up_recv, down_send, down_recv, side_send, side_recv,
    swap_send, swap_recv, red_up_send, red_up_recv, red_down_send, red_down_recv,
):
    near = ring - 1 - far
    me = lax.axis_index("batch")
    y, c = me // 2, me % 2
    way = 1 - 2 * c
    other = y * 2 + (1 - c)

    def at(k):
        return lax.rem(y + k * way + ring, ring)

    def mine(k):
        return at(k) * 2 + c

    def theirs(k):
        return at(k) * 2 + (1 - c)

    def values(r):
        return pltpu.make_async_copy(basis_ref.at[r], phi_ref.at[r], load.at[r])

    for r in range(regions):
        values(r).start()
    barrier = pltpu.get_barrier_semaphore()
    for target in (mine(1), mine(-1), other):
        pl.semaphore_signal(barrier, inc=1, device_id={"batch": target}, device_id_type=MESH)
    pl.semaphore_wait(barrier, 3)

    def remote(src, dst, send, recv, target):
        return pltpu.make_async_remote_copy(
            src_ref=src, dst_ref=dst, send_sem=send, recv_sem=recv,
            device_id={"batch": target}, device_id_type=MESH,
        )

    def part(r):
        return pl.ds(3 * r, 3)

    def block(r, slot):
        return tiles.at[part(r), slot]

    def up_hop(a, r):
        src = own_ref.at[part(r)] if a == 0 else block(r, mine(-a))
        return remote(src, block(r, mine(-a)), up_send.at[a, r], up_recv.at[a, r], mine(1))

    def up_arrival(a, r):
        slot = block(r, mine(-(a + 1)))
        return remote(slot, slot, up_send.at[a, r], up_recv.at[a, r], mine(1))

    def down_hop(a, r):
        src = own_ref.at[part(r)] if a == 0 else block(r, mine(a))
        return remote(src, block(r, mine(a)), down_send.at[a, r], down_recv.at[a, r], mine(-1))

    def down_arrival(a, r):
        slot = block(r, mine(a + 1))
        return remote(slot, slot, down_send.at[a, r], down_recv.at[a, r], mine(-1))

    def side(i, r):
        if i == 0:
            src, slot = own_ref.at[part(r)], block(r, me)
        else:
            slot = block(r, mine(-i if i <= far else i - far))
            src = slot
        return remote(src, slot, side_send.at[i, r], side_recv.at[i, r], other)

    def side_arrival(i, r):
        k = 0 if i == 0 else (i if i <= far else far - i)
        slot = block(r, theirs(k))
        return remote(slot, slot, side_send.at[i, r], side_recv.at[i, r], other)

    def gather_step(a, r):
        if a == 0:
            up_hop(0, r).start()
            down_hop(0, r).start()
            side(0, r).start()
            tiles[part(r), me] = own_ref[part(r)]
            return
        up_arrival(a - 1, r).wait_recv()
        if a < far:
            up_hop(a, r).start()
        side(a, r).start()
        if a <= near:
            down_arrival(a - 1, r).wait_recv()
            if a < near:
                down_hop(a, r).start()
            side(far + a, r).start()

    def swap(r):
        return remote(
            pairs.at[part(r), :, 1 - c], peer.at[part(r)],
            swap_send.at[r], swap_recv.at[r], other,
        )

    def compute(r):
        for i in range(ring):
            side_arrival(i, r).wait_recv()
        values(r).wait()
        width = phi_ref.shape[-1]
        phi_a, phi_b = phi_ref[r, 0], phi_ref[r, 1]

        def left(phi, j):
            matrix = tiles[3 * r + j].reshape(2 * ring * rows, width)
            return jnp.dot(phi, matrix, preferred_element_type=jnp.float32)

        wide_a, wide_b = phi_a.astype(jnp.float32), phi_b.astype(jnp.float32)
        density = jnp.sum(
            wide_a * left(phi_a, 0) + wide_b * (2.0 * left(phi_a, 1) + left(phi_b, 2)),
            axis=1, keepdims=True,
        )
        scale = weight_ref[r] * potential(density)
        scaled_a = (scale * wide_a).astype(jnp.bfloat16)
        scaled_b = (scale * wide_b).astype(jnp.bfloat16)
        for j, (lhs, rhs) in enumerate(((phi_a, scaled_a), (phi_a, scaled_b), (phi_b, scaled_b))):
            product = lax.dot_general(
                lhs, rhs, (((0,), (0,)), ((), ())), preferred_element_type=jnp.float32
            )
            pairs[3 * r + j] = product.astype(jnp.bfloat16).reshape(ring, 2, rows, width)
        swap(r).start()

    def chip_sum(r, k):
        return pairs[part(r), at(k), c].astype(jnp.float32) + peer[part(r), at(k)].astype(jnp.float32)

    def red_up(s, r):
        return remote(
            sum_up.at[s, part(r)], got_up.at[s, part(r)],
            red_up_send.at[s, r], red_up_recv.at[s, r], mine(1),
        )

    def red_down(s, r):
        return remote(
            sum_down.at[s, part(r)], got_down.at[s, part(r)],
            red_down_send.at[s, r], red_down_recv.at[s, r], mine(-1),
        )

    def reduce_step(s, r):
        if s == 0:
            swap(r).wait_recv()
        total = chip_sum(r, far - s)
        if s > 0:
            red_up(s - 1, r).wait_recv()
            total = total + got_up[s - 1, part(r)].astype(jnp.float32)
        sum_up[s, part(r)] = total.astype(jnp.bfloat16)
        red_up(s, r).start()
        if s < near:
            total = chip_sum(r, s - near)
            if s > 0:
                red_down(s - 1, r).wait_recv()
                total = total + got_down[s - 1, part(r)].astype(jnp.float32)
            sum_down[s, part(r)] = total.astype(jnp.bfloat16)
            red_down(s, r).start()

    def finish(r):
        red_up(far - 1, r).wait_recv()
        red_down(near - 1, r).wait_recv()
        total = chip_sum(r, 0)
        total = total + got_up[far - 1, part(r)].astype(jnp.float32)
        total = total + got_down[near - 1, part(r)].astype(jnp.float32)
        out_ref[part(r)] = total.astype(out_ref.dtype)

    for action, *where in schedule(far, near, regions):
        (gather_step, compute, reduce_step, finish)[action](*where)

    for r in range(regions):
        for a in range(far):
            up_hop(a, r).wait_send()
            red_up(a, r).wait_send()
        for a in range(near):
            down_hop(a, r).wait_send()
            red_down(a, r).wait_send()
        for i in range(ring):
            side(i, r).wait_send()
        swap(r).wait_send()


def over_batch(fetched, basis_values, weights, batch_count):
    ring = batch_count // 2
    far = ring // 2
    near = ring - 1 - far
    regions = basis_values.shape[0]
    requests, rows, width = fetched.shape
    dma = pltpu.SemaphoreType.DMA
    half = jnp.bfloat16
    vmem = pl.BlockSpec(memory_space=pltpu.VMEM)
    return pl.pallas_call(
        functools.partial(batch_kernel, ring, far, regions, rows),
        out_shape=jax.ShapeDtypeStruct((requests, rows, width), half),
        in_specs=[vmem, pl.BlockSpec(memory_space=pltpu.HBM), vmem],
        out_specs=vmem,
        scratch_shapes=[
            pltpu.VMEM(basis_values.shape, half), dma((regions,)),
            pltpu.VMEM((requests, batch_count, rows, width), half),
            pltpu.VMEM((requests, ring, 2, rows, width), half),
            pltpu.VMEM((requests, ring, rows, width), half),
            pltpu.VMEM((far, requests, rows, width), half),
            pltpu.VMEM((far, requests, rows, width), half),
            pltpu.VMEM((near, requests, rows, width), half),
            pltpu.VMEM((near, requests, rows, width), half),
            dma((far, regions)), dma((far, regions)),
            dma((near, regions)), dma((near, regions)),
            dma((ring, regions)), dma((ring, regions)),
            dma((regions,)), dma((regions,)),
            dma((far, regions)), dma((far, regions)),
            dma((near, regions)), dma((near, regions)),
        ],
        compiler_params=pltpu.CompilerParams(
            collective_id=0, has_side_effects=True, vmem_limit_bytes=52 * 1024 * 1024
        ),
        name="over_batch",
    )(fetched, basis_values, weights)


def plane(columns, ring):
    m = lax.axis_index("region")
    x, z = m // ring, m % ring
    way = 1 - 2 * (lax.axis_index("batch") % 2)

    def at(k):
        return lax.rem(z + k * way + ring, ring)

    def along_z(k):
        return x * ring + at(k)

    def along_x(d):
        return lax.rem(x + d + columns, columns) * ring + z

    def greet():
        barrier = pltpu.get_barrier_semaphore()
        targets = [along_z(1), along_z(-1)] + [along_x(d) for d in range(1, columns)]
        for target in targets:
            pl.semaphore_signal(barrier, inc=1, device_id={"region": target}, device_id_type=MESH)
        pl.semaphore_wait(barrier, len(targets))

    return x, way, at, along_z, along_x, greet


def to_region(src, dst, send, recv, target):
    return pltpu.make_async_remote_copy(
        src_ref=src, dst_ref=dst, send_sem=send, recv_sem=recv,
        device_id={"region": target}, device_id_type=MESH,
    )


def fetch_kernel(columns, ring, far, table_ref, owner_ref, own_ref, out_ref, stage, landed,
                 up_send, up_recv, down_send, down_recv, x_send, x_recv, relay, relay_send, relay_recv,
                 *held):
    near = ring - 1 - far
    kept = own_ref.shape[0]
    x, way, at, along_z, along_x, greet = plane(columns, ring)
    greet()

    def source(i):
        return own_ref if i == 0 else held[i - 1]

    def place(i):
        return 0 if i == 0 else (-i if i <= far else i - far)

    def up(a, t):
        return to_region(source(a).at[t], held[a].at[t], up_send.at[a, t], up_recv.at[a, t], along_z(1))

    def down(a, t):
        src = own_ref if a == 0 else held[far + a - 1]
        return to_region(
            src.at[t], held[far + a].at[t], down_send.at[a, t], down_recv.at[a, t], along_z(-1)
        )

    def across(d, i):
        return to_region(
            stage.at[d - 1, i], landed.at[along_z(place(i))],
            x_send.at[d - 1, i], x_recv.at[d - 1, i], along_x(d),
        )

    def arrival(d, i):
        slot = landed.at[lax.rem(x + columns - d, columns) * ring + at(place(i))]
        return to_region(slot, slot, x_send.at[d - 1, i], x_recv.at[d - 1, i], along_x(d))

    def first_leg(i):
        return to_region(stage.at[1, i], relay.at[i], relay_send.at[i], relay_recv.at[i], along_x(way))

    def second_leg(i):
        column = lax.rem(x - way + columns, columns)
        return to_region(
            relay.at[i], landed.at[column * ring + at(place(i))],
            x_send.at[1, i], x_recv.at[1, i], along_x(way),
        )

    def hand_on(i):
        slot = relay.at[i]
        to_region(slot, slot, relay_send.at[i], relay_recv.at[i], along_x(way)).wait_recv()
        second_leg(i).start()

    def pass_on(i):
        zo = at(place(i))
        for d in range(1, columns):
            wanted = jnp.maximum(table_ref[lax.rem(x + d, columns), zo], 0)
            stage[d - 1, i] = source(i)[wanted]
            (first_leg(i) if d == 2 else across(d, i)).start()
        landed[along_z(place(i))] = source(i)[jnp.maximum(table_ref[x, zo], 0)]

    for t in range(kept):
        up(0, t).start()
        down(0, t).start()
    pass_on(0)
    for a in range(1, far + 1):
        for t in range(kept):
            up(a - 1, t).wait_recv()
            if a < far:
                up(a, t).start()
            if a <= near:
                down(a - 1, t).wait_recv()
                if a < near:
                    down(a, t).start()
        pass_on(a)
        if a <= near:
            pass_on(far + a)
        hand_on(a - 1)
        if a > 1:
            hand_on(far + a - 1)
    hand_on(far)
    for i in range(ring):
        for d in range(1, columns):
            arrival(d, i).wait_recv()
    for j in range(out_ref.shape[0]):
        out_ref[j] = landed[owner_ref[j]]
    for t in range(kept):
        for a in range(far):
            up(a, t).wait_send()
        for a in range(near):
            down(a, t).wait_send()
    for i in range(ring):
        for d in range(1, columns):
            (second_leg(i) if d == 2 else across(d, i)).wait_send()
        first_leg(i).wait_send()


def give_kernel(columns, ring, far, table_ref, request_ref, pairs_ref, out_ref, stage, landed,
                sum_up, got_up, sum_down, got_down,
                up_send, up_recv, down_send, down_recv, x_send, x_recv, relay, relay_send, relay_recv):
    near = ring - 1 - far
    kept = out_ref.shape[0]
    x, way, at, along_z, along_x, greet = plane(columns, ring)
    greet()

    def across(d, i):
        return to_region(
            stage.at[d - 1, i], landed.at[d - 1, i], x_send.at[d - 1, i], x_recv.at[d - 1, i], along_x(d)
        )

    def up(s, t):
        return to_region(sum_up.at[s, t], got_up.at[s, t], up_send.at[s, t], up_recv.at[s, t], along_z(1))

    def down(s, t):
        return to_region(
            sum_down.at[s, t], got_down.at[s, t], down_send.at[s, t], down_recv.at[s, t], along_z(-1)
        )

    def first_leg(i):
        return to_region(stage.at[1, i], relay.at[i], relay_send.at[i], relay_recv.at[i], along_x(way))

    def second_leg(i):
        return to_region(relay.at[i], landed.at[1, i], x_send.at[1, i], x_recv.at[1, i], along_x(way))

    def hand_on(i):
        slot = relay.at[i]
        to_region(slot, slot, relay_send.at[i], relay_recv.at[i], along_x(way)).wait_recv()
        second_leg(i).start()

    order = []
    for s in range(far):
        order.append(far - s)
        if s < near:
            order.append(s - near)
    order.append(0)
    for k in order:
        for d in range(1, columns):
            request = request_ref[lax.rem(x + d, columns), at(k)]
            stage[d - 1, k % ring] = pairs_ref[request]
            (first_leg(k % ring) if d == 2 else across(d, k % ring)).start()
    hand_on(order[0] % ring)
    hand_on(order[1] % ring)

    def placed(k):
        ahead = order.index(k) + 2
        if ahead < ring:
            hand_on(order[ahead] % ring)
        for d in range(1, columns):
            across(d, k % ring).wait_recv()
        terms = [(table_ref[x, at(k)], pairs_ref[request_ref[x, at(k)]].astype(jnp.float32))]
        for d in range(1, columns):
            sender = lax.rem(x + columns - d, columns)
            terms.append((table_ref[sender, at(k)], landed[d - 1, k % ring].astype(jnp.float32)))

        def tile(t):
            total = jnp.zeros(pairs_ref.shape[1:], jnp.float32)
            for wanted, values in terms:
                total = total + jnp.where(jnp.full(values.shape, wanted, jnp.int32) == t, values, 0.0)
            return total

        return tile

    for s in range(far):
        tile = placed(far - s)
        for t in range(kept):
            total = tile(t)
            if s > 0:
                up(s - 1, t).wait_recv()
                total = total + got_up[s - 1, t].astype(jnp.float32)
            sum_up[s, t] = total.astype(sum_up.dtype)
            up(s, t).start()
        if s < near:
            tile = placed(s - near)
            for t in range(kept):
                total = tile(t)
                if s > 0:
                    down(s - 1, t).wait_recv()
                    total = total + got_down[s - 1, t].astype(jnp.float32)
                sum_down[s, t] = total.astype(sum_down.dtype)
                down(s, t).start()
    tile = placed(0)
    for t in range(kept):
        total = tile(t)
        down(near - 1, t).wait_recv()
        total = total + got_down[near - 1, t].astype(jnp.float32)
        up(far - 1, t).wait_recv()
        out_ref[t] = total + got_up[far - 1, t].astype(jnp.float32)
    for t in range(kept):
        for s in range(far):
            up(s, t).wait_send()
        for s in range(near):
            down(s, t).wait_send()
    for i in range(ring):
        for d in range(1, columns):
            (second_leg(i) if d == 2 else across(d, i)).wait_send()
        first_leg(i).wait_send()


def over_region(kernel, name, collective_id, scratch, out, columns, ring, far, table, index, values):
    vmem, smem = pl.BlockSpec(memory_space=pltpu.VMEM), pl.BlockSpec(memory_space=pltpu.SMEM)
    return pl.pallas_call(
        functools.partial(kernel, columns, ring, far),
        out_shape=out,
        in_specs=[smem, smem, vmem],
        out_specs=vmem,
        scratch_shapes=scratch,
        compiler_params=pltpu.CompilerParams(
            collective_id=collective_id, has_side_effects=True, vmem_limit_bytes=32 * 1024 * 1024
        ),
        name=name,
    )(table, index, values)


COLUMNS = 4


def plane_semaphores(columns, ring, far, kept):
    dma = pltpu.SemaphoreType.DMA
    near = ring - 1 - far
    return [
        dma((far, kept)), dma((far, kept)), dma((near, kept)), dma((near, kept)),
        dma((columns - 1, ring)), dma((columns - 1, ring)),
    ]


def relay_scratch(ring, rows, width, kind):
    dma = pltpu.SemaphoreType.DMA
    return [pltpu.VMEM((ring, rows, width), kind), dma((ring,)), dma((ring,))]


def fetch(table, my_owners, dens_tiles, ring):
    far = ring // 2
    kept, rows, width = dens_tiles.shape
    kind = dens_tiles.dtype
    scratch = [
        pltpu.VMEM((COLUMNS - 1, ring, rows, width), kind),
        pltpu.VMEM((COLUMNS * ring, rows, width), kind),
    ]
    scratch += plane_semaphores(COLUMNS, ring, far, kept)
    scratch += relay_scratch(ring, rows, width, kind)
    scratch += [pltpu.VMEM((kept, rows, width), kind)] * (ring - 1)
    out = jax.ShapeDtypeStruct((my_owners.shape[0], rows, width), kind)
    return over_region(
        fetch_kernel, "fetch", 1, scratch, out, COLUMNS, ring, far, table, my_owners, dens_tiles
    )


def give(table, request, pairs, kept, ring):
    far = ring // 2
    near = ring - 1 - far
    rows, width = pairs.shape[1:]
    kind = pairs.dtype
    scratch = [pltpu.VMEM((COLUMNS - 1, ring, rows, width), kind)] * 2
    scratch += [pltpu.VMEM((far, kept, rows, width), kind)] * 2
    scratch += [pltpu.VMEM((near, kept, rows, width), kind)] * 2
    scratch += plane_semaphores(COLUMNS, ring, far, kept)
    scratch += relay_scratch(ring, rows, width, kind)
    out = jax.ShapeDtypeStruct((kept, rows, width), jnp.float32)
    return over_region(
        give_kernel, "give", 2, scratch, out, COLUMNS, ring, far, table, request, pairs
    )


def shards(basis_values, dens_tiles, region_tiles, point_counts, point_weights):
    owner_count = lax.axis_size("region")
    batch_count = lax.axis_size("batch")
    ring = owner_count // COLUMNS
    my_index = lax.axis_index("region")
    region_local = basis_values.shape[0]
    point_local = basis_values.shape[2]
    tile_local = dens_tiles.shape[0]
    requests = 3 * region_local
    owners = region_tiles.reshape(owner_count, requests) // tile_local
    local_ids = region_tiles.reshape(owner_count, requests) % tile_local
    mine = owners[:, :, None] == jnp.arange(owner_count, dtype=jnp.int32)
    wanted = jnp.sum(jnp.where(mine, local_ids[:, :, None] + 1, 0), axis=1) - 1
    order = jnp.arange(requests, dtype=jnp.int32)
    request_of = jnp.sum(jnp.where(mine, order[None, :, None], 0), axis=1)
    my_owners = lax.dynamic_index_in_dim(owners, my_index, 0, keepdims=False)
    request = lax.dynamic_index_in_dim(request_of, my_index, 0, keepdims=False)
    request = request.reshape(COLUMNS, ring)
    table = wanted.reshape(COLUMNS, ring, COLUMNS, ring)
    table = lax.dynamic_index_in_dim(table, my_index % ring, 1, keepdims=False)
    table = lax.dynamic_index_in_dim(table, my_index // ring, 1, keepdims=False)
    fetched = fetch(table, my_owners, dens_tiles, ring)
    live = jnp.arange(point_local, dtype=jnp.int32)[None, :] < point_counts
    weights = jnp.where(live, point_weights, 0.0)[:, :, None]
    pairs = over_batch(fetched, basis_values, weights, batch_count)
    return give(table, request, pairs, tile_local, ring)


def solution(mesh):
    return jax.shard_map(
        shards,
        mesh=mesh,
        in_specs=(
            P("region", None, "batch", None),
            P("region", "batch", None),
            P(),
            P("region", "batch"),
            P("region", "batch"),
        ),
        out_specs=P("region", "batch", None),
        check_vma=False,
    )
```

```python
import functools

import jax
import jax.numpy as jnp
from jax import lax
from jax.experimental import pallas as pl
from jax.experimental.pallas import tpu as pltpu
from jax.sharding import PartitionSpec as P

SLATER = 0.9847450218426964
MESH = pl.DeviceIdType.MESH


def potential(density):
    return -SLATER * density * jnp.exp(jnp.log(density * density + 1.0) * (-1.0 / 3.0))


GATHER, COMPUTE, REDUCE, FINISH = range(4)


def schedule(far, near, regions):
    if (far, regions) != (4, 4):
        order = [(GATHER, a, r) for a in range(far + 1) for r in range(regions)]
        order += [(COMPUTE, r) for r in range(regions)]
        order += [(REDUCE, s, r) for s in range(far) for r in range(regions)]
        return order + [(FINISH, r) for r in range(regions)]
    order = []
    for t in range(5):
        order += [(GATHER, t, 0), (GATHER, t, 1)]
        if t >= 2:
            order += [(GATHER, t - 2, 2), (GATHER, t - 2, 3)]
    order += [(COMPUTE, 0), (GATHER, 3, 2), (GATHER, 3, 3), (COMPUTE, 1), (REDUCE, 0, 0)]
    order += [(GATHER, 4, 2), (REDUCE, 0, 1), (GATHER, 4, 3), (REDUCE, 1, 0), (COMPUTE, 2)]
    order += [(REDUCE, 1, 1), (REDUCE, 2, 0), (REDUCE, 0, 2), (COMPUTE, 3), (REDUCE, 1, 2)]
    order += [(REDUCE, 2, 1), (REDUCE, 3, 0), (REDUCE, 0, 3), (REDUCE, 2, 2), (REDUCE, 3, 1)]
    order += [(REDUCE, 1, 3), (FINISH, 0), (REDUCE, 3, 2), (REDUCE, 2, 3), (FINISH, 1)]
    return order + [(REDUCE, 3, 3), (FINISH, 2), (FINISH, 3)]


def batch_kernel(
    ring, far, regions, rows, own_ref, basis_ref, weight_ref, out_ref,
    phi_ref, load, tiles, pairs, peer, sum_up, got_up, sum_down, got_down,
    up_send, up_recv, down_send, down_recv, side_send, side_recv,
    swap_send, swap_recv, red_up_send, red_up_recv, red_down_send, red_down_recv,
):
    near = ring - 1 - far
    me = lax.axis_index("batch")
    y, c = me // 2, me % 2
    way = 1 - 2 * c
    other = y * 2 + (1 - c)

    def at(k):
        return lax.rem(y + k * way + ring, ring)

    def mine(k):
        return at(k) * 2 + c

    def theirs(k):
        return at(k) * 2 + (1 - c)

    def values(r):
        return pltpu.make_async_copy(basis_ref.at[r], phi_ref.at[r], load.at[r])

    for r in range(regions):
        values(r).start()
    def remote(src, dst, send, recv, target):
        return pltpu.make_async_remote_copy(
            src_ref=src, dst_ref=dst, send_sem=send, recv_sem=recv,
            device_id={"batch": target}, device_id_type=MESH,
        )

    def part(r):
        return pl.ds(3 * r, 3)

    def block(r, slot):
        return tiles.at[part(r), slot]

    def up_hop(a, r):
        src = own_ref.at[part(r)] if a == 0 else block(r, mine(-a))
        return remote(src, block(r, mine(-a)), up_send.at[a, r], up_recv.at[a, r], mine(1))

    def up_arrival(a, r):
        slot = block(r, mine(-(a + 1)))
        return remote(slot, slot, up_send.at[a, r], up_recv.at[a, r], mine(1))

    def down_hop(a, r):
        src = own_ref.at[part(r)] if a == 0 else block(r, mine(a))
        return remote(src, block(r, mine(a)), down_send.at[a, r], down_recv.at[a, r], mine(-1))

    def down_arrival(a, r):
        slot = block(r, mine(a + 1))
        return remote(slot, slot, down_send.at[a, r], down_recv.at[a, r], mine(-1))

    def side(i, r):
        if i == 0:
            src, slot = own_ref.at[part(r)], block(r, me)
        else:
            slot = block(r, mine(-i if i <= far else i - far))
            src = slot
        return remote(src, slot, side_send.at[i, r], side_recv.at[i, r], other)

    def side_arrival(i, r):
        k = 0 if i == 0 else (i if i <= far else far - i)
        slot = block(r, theirs(k))
        return remote(slot, slot, side_send.at[i, r], side_recv.at[i, r], other)

    def gather_step(a, r):
        if a == 0:
            up_hop(0, r).start()
            down_hop(0, r).start()
            side(0, r).start()
            tiles[part(r), me] = own_ref[part(r)]
            return
        up_arrival(a - 1, r).wait_recv()
        if a < far:
            up_hop(a, r).start()
        side(a, r).start()
        if a <= near:
            down_arrival(a - 1, r).wait_recv()
            if a < near:
                down_hop(a, r).start()
            side(far + a, r).start()

    def swap(r):
        return remote(
            pairs.at[part(r), :, 1 - c], peer.at[part(r)],
            swap_send.at[r], swap_recv.at[r], other,
        )

    def compute(r):
        for i in range(ring):
            side_arrival(i, r).wait_recv()
        values(r).wait()
        width = phi_ref.shape[-1]
        phi_a, phi_b = phi_ref[r, 0], phi_ref[r, 1]

        def left(phi, j):
            matrix = tiles[3 * r + j].reshape(2 * ring * rows, width)
            return jnp.dot(phi, matrix, preferred_element_type=jnp.float32)

        wide_a, wide_b = phi_a.astype(jnp.float32), phi_b.astype(jnp.float32)
        density = jnp.sum(
            wide_a * left(phi_a, 0) + wide_b * (2.0 * left(phi_a, 1) + left(phi_b, 2)),
            axis=1, keepdims=True,
        )
        scale = weight_ref[r] * potential(density)
        scaled_a = (scale * wide_a).astype(jnp.bfloat16)
        scaled_b = (scale * wide_b).astype(jnp.bfloat16)
        for j, (lhs, rhs) in enumerate(((phi_a, scaled_a), (phi_a, scaled_b), (phi_b, scaled_b))):
            product = lax.dot_general(
                lhs, rhs, (((0,), (0,)), ((), ())), preferred_element_type=jnp.float32
            )
            pairs[3 * r + j] = product.astype(jnp.bfloat16).reshape(ring, 2, rows, width)
        swap(r).start()

    def chip_sum(r, k):
        return pairs[part(r), at(k), c].astype(jnp.float32) + peer[part(r), at(k)].astype(jnp.float32)

    def red_up(s, r):
        return remote(
            sum_up.at[s, part(r)], got_up.at[s, part(r)],
            red_up_send.at[s, r], red_up_recv.at[s, r], mine(1),
        )

    def red_down(s, r):
        return remote(
            sum_down.at[s, part(r)], got_down.at[s, part(r)],
            red_down_send.at[s, r], red_down_recv.at[s, r], mine(-1),
        )

    def reduce_step(s, r):
        if s == 0:
            swap(r).wait_recv()
        total = chip_sum(r, far - s)
        if s > 0:
            red_up(s - 1, r).wait_recv()
            total = total + got_up[s - 1, part(r)].astype(jnp.float32)
        sum_up[s, part(r)] = total.astype(jnp.bfloat16)
        red_up(s, r).start()
        if s < near:
            total = chip_sum(r, s - near)
            if s > 0:
                red_down(s - 1, r).wait_recv()
                total = total + got_down[s - 1, part(r)].astype(jnp.float32)
            sum_down[s, part(r)] = total.astype(jnp.bfloat16)
            red_down(s, r).start()

    def finish(r):
        red_up(far - 1, r).wait_recv()
        red_down(near - 1, r).wait_recv()
        total = chip_sum(r, 0)
        total = total + got_up[far - 1, part(r)].astype(jnp.float32)
        total = total + got_down[near - 1, part(r)].astype(jnp.float32)
        out_ref[part(r)] = total.astype(out_ref.dtype)

    for action, *where in schedule(far, near, regions):
        (gather_step, compute, reduce_step, finish)[action](*where)

    def drain():
        for r in range(regions):
            for a in range(far):
                up_hop(a, r).wait_send()
                red_up(a, r).wait_send()
            for a in range(near):
                down_hop(a, r).wait_send()
                red_down(a, r).wait_send()
            for i in range(ring):
                side(i, r).wait_send()
            swap(r).wait_send()

    return drain


def batch_scratch(basis_values, requests, rows, batch_count):
    ring = batch_count // 2
    far = ring // 2
    near = ring - 1 - far
    regions, _, _, width = basis_values.shape
    dma = pltpu.SemaphoreType.DMA
    half = jnp.bfloat16
    return [
        pltpu.VMEM(basis_values.shape, half), dma((regions,)),
        pltpu.VMEM((requests, batch_count, rows, width), half),
        pltpu.VMEM((requests, ring, 2, rows, width), half),
        pltpu.VMEM((requests, ring, rows, width), half),
        pltpu.VMEM((far, requests, rows, width), half),
        pltpu.VMEM((far, requests, rows, width), half),
        pltpu.VMEM((near, requests, rows, width), half),
        pltpu.VMEM((near, requests, rows, width), half),
        dma((far, regions)), dma((far, regions)),
        dma((near, regions)), dma((near, regions)),
        dma((ring, regions)), dma((ring, regions)),
        dma((regions,)), dma((regions,)),
        dma((far, regions)), dma((far, regions)),
        dma((near, regions)), dma((near, regions)),
    ]


def plane(columns, ring):
    m = lax.axis_index("region")
    x, z = m // ring, m % ring
    way = 1 - 2 * (lax.axis_index("batch") % 2)

    def at(k):
        return lax.rem(z + k * way + ring, ring)

    def along_z(k):
        return x * ring + at(k)

    def along_x(d):
        return lax.rem(x + d, columns) * ring + z

    return x, at, along_z, along_x


def to_region(src, dst, send, recv, target):
    return pltpu.make_async_remote_copy(
        src_ref=src, dst_ref=dst, send_sem=send, recv_sem=recv,
        device_id={"region": target}, device_id_type=MESH,
    )


def fetch_kernel(columns, ring, far, table_ref, owner_ref, own_ref, out_ref, stage, landed,
                 up_send, up_recv, down_send, down_recv, x_send, x_recv, *held):
    near = ring - 1 - far
    kept = own_ref.shape[0]
    x, at, along_z, along_x = plane(columns, ring)
    def source(i):
        return own_ref if i == 0 else held[i - 1]

    def place(i):
        return 0 if i == 0 else (-i if i <= far else i - far)

    def up(a, t):
        return to_region(source(a).at[t], held[a].at[t], up_send.at[a, t], up_recv.at[a, t], along_z(1))

    def down(a, t):
        src = own_ref if a == 0 else held[far + a - 1]
        return to_region(
            src.at[t], held[far + a].at[t], down_send.at[a, t], down_recv.at[a, t], along_z(-1)
        )

    def across(d, i):
        return to_region(
            stage.at[d - 1, i], landed.at[along_z(place(i))],
            x_send.at[d - 1, i], x_recv.at[d - 1, i], along_x(d),
        )

    def arrival(d, i):
        slot = landed.at[lax.rem(x + columns - d, columns) * ring + at(place(i))]
        return to_region(slot, slot, x_send.at[d - 1, i], x_recv.at[d - 1, i], along_x(d))

    def pass_on(i):
        zo = at(place(i))
        for d in range(1, columns):
            wanted = jnp.maximum(table_ref[lax.rem(x + d, columns), zo], 0)
            stage[d - 1, i] = source(i)[wanted]
            across(d, i).start()
        landed[along_z(place(i))] = source(i)[jnp.maximum(table_ref[x, zo], 0)]

    for t in range(kept):
        up(0, t).start()
        down(0, t).start()
    pass_on(0)
    for a in range(1, far + 1):
        for t in range(kept):
            up(a - 1, t).wait_recv()
            if a < far:
                up(a, t).start()
            if a <= near:
                down(a - 1, t).wait_recv()
                if a < near:
                    down(a, t).start()
        pass_on(a)
        if a <= near:
            pass_on(far + a)
    for i in range(ring):
        for d in range(1, columns):
            arrival(d, i).wait_recv()
    for j in range(out_ref.shape[0]):
        out_ref[j] = landed[owner_ref[j]]

    def drain():
        for t in range(kept):
            for a in range(far):
                up(a, t).wait_send()
            for a in range(near):
                down(a, t).wait_send()
        for i in range(ring):
            for d in range(1, columns):
                across(d, i).wait_send()

    return drain


def give_kernel(columns, ring, far, table_ref, request_ref, pairs_ref, out_ref, stage, landed,
                sum_up, got_up, sum_down, got_down,
                up_send, up_recv, down_send, down_recv, x_send, x_recv):
    near = ring - 1 - far
    kept = out_ref.shape[0]
    x, at, along_z, along_x = plane(columns, ring)
    def across(d, i):
        return to_region(
            stage.at[d - 1, i], landed.at[d - 1, i], x_send.at[d - 1, i], x_recv.at[d - 1, i], along_x(d)
        )

    def up(s, t):
        return to_region(sum_up.at[s, t], got_up.at[s, t], up_send.at[s, t], up_recv.at[s, t], along_z(1))

    def down(s, t):
        return to_region(
            sum_down.at[s, t], got_down.at[s, t], down_send.at[s, t], down_recv.at[s, t], along_z(-1)
        )

    order = []
    for s in range(far):
        order.append(far - s)
        if s < near:
            order.append(s - near)
    order.append(0)
    for k in order:
        for d in range(1, columns):
            request = request_ref[lax.rem(x + d, columns), at(k)]
            stage[d - 1, k % ring] = pairs_ref[request]
            across(d, k % ring).start()

    def placed(k):
        for d in range(1, columns):
            across(d, k % ring).wait_recv()
        terms = [(table_ref[x, at(k)], pairs_ref[request_ref[x, at(k)]].astype(jnp.float32))]
        for d in range(1, columns):
            sender = lax.rem(x + columns - d, columns)
            terms.append((table_ref[sender, at(k)], landed[d - 1, k % ring].astype(jnp.float32)))

        def tile(t):
            total = jnp.zeros(pairs_ref.shape[1:], jnp.float32)
            for wanted, values in terms:
                total = total + jnp.where(jnp.full(values.shape, wanted, jnp.int32) == t, values, 0.0)
            return total

        return tile

    for s in range(far):
        tile = placed(far - s)
        for t in range(kept):
            total = tile(t)
            if s > 0:
                up(s - 1, t).wait_recv()
                total = total + got_up[s - 1, t].astype(jnp.float32)
            sum_up[s, t] = total.astype(sum_up.dtype)
            up(s, t).start()
        if s < near:
            tile = placed(s - near)
            for t in range(kept):
                total = tile(t)
                if s > 0:
                    down(s - 1, t).wait_recv()
                    total = total + got_down[s - 1, t].astype(jnp.float32)
                sum_down[s, t] = total.astype(sum_down.dtype)
                down(s, t).start()
    tile = placed(0)
    for t in range(kept):
        total = tile(t)
        down(near - 1, t).wait_recv()
        total = total + got_down[near - 1, t].astype(jnp.float32)
        up(far - 1, t).wait_recv()
        out_ref[t] = total + got_up[far - 1, t].astype(jnp.float32)
    for t in range(kept):
        for s in range(far):
            up(s, t).wait_send()
        for s in range(near):
            down(s, t).wait_send()
    for k in order:
        for d in range(1, columns):
            across(d, k % ring).wait_send()


COLUMNS = 4


def plane_semaphores(columns, ring, far, kept):
    dma = pltpu.SemaphoreType.DMA
    near = ring - 1 - far
    return [
        dma((far, kept)), dma((far, kept)), dma((near, kept)), dma((near, kept)),
        dma((columns - 1, ring)), dma((columns - 1, ring)),
    ]


def fetch_scratch(ring, kept, rows, width, kind):
    scratch = [
        pltpu.VMEM((COLUMNS - 1, ring, rows, width), kind),
        pltpu.VMEM((COLUMNS * ring, rows, width), kind),
    ]
    scratch += plane_semaphores(COLUMNS, ring, ring // 2, kept)
    return scratch + [pltpu.VMEM((kept, rows, width), kind)] * (ring - 1)


def give_scratch(ring, kept, rows, width, kind):
    far = ring // 2
    near = ring - 1 - far
    scratch = [pltpu.VMEM((COLUMNS - 1, ring, rows, width), kind)] * 2
    scratch += [pltpu.VMEM((far, kept, rows, width), kind)] * 2
    scratch += [pltpu.VMEM((near, kept, rows, width), kind)] * 2
    return scratch + plane_semaphores(COLUMNS, ring, far, kept)


def whole_kernel(ring, y_ring, regions, rows, counts, table_ref, owner_ref, request_ref, dens_ref,
                 basis_ref, weight_ref, out_ref, fetched, pairs, *scratch):
    x, at, along_z, along_x = plane(COLUMNS, ring)
    me = lax.axis_index("batch")
    barrier = pltpu.get_barrier_semaphore()
    targets = [{"region": along_z(1)}, {"region": along_z(-1)}]
    targets += [{"region": along_x(d)} for d in range(1, COLUMNS)]
    targets += [{"batch": lax.rem(me + k, 2 * y_ring)} for k in (2, 2 * y_ring - 2)]
    targets += [{"batch": me // 2 * 2 + 1 - me % 2}]
    for target in targets:
        pl.semaphore_signal(barrier, inc=1, device_id=target, device_id_type=MESH)
    pl.semaphore_wait(barrier, len(targets))
    first, second = counts
    drains = [
        fetch_kernel(COLUMNS, ring, ring // 2, table_ref, owner_ref, dens_ref, fetched, *scratch[:first]),
        batch_kernel(y_ring, y_ring // 2, regions, rows, fetched, basis_ref, weight_ref, pairs,
                     *scratch[first:second]),
    ]
    give_kernel(COLUMNS, ring, ring // 2, table_ref, request_ref, pairs, out_ref, *scratch[second:])
    for drain in drains:
        drain()


def exchange(table, my_owners, request, dens_tiles, basis_values, weights, ring, batch_count):
    kept, rows, width = dens_tiles.shape
    kind = dens_tiles.dtype
    requests = my_owners.shape[0]
    regions = basis_values.shape[0]
    first = fetch_scratch(ring, kept, rows, width, kind)
    second = batch_scratch(basis_values, requests, rows, batch_count)
    third = give_scratch(ring, kept, rows, width, kind)
    counts = (len(first), len(first) + len(second))
    vmem, smem = pl.BlockSpec(memory_space=pltpu.VMEM), pl.BlockSpec(memory_space=pltpu.SMEM)
    return pl.pallas_call(
        functools.partial(whole_kernel, ring, batch_count // 2, regions, rows, counts),
        out_shape=jax.ShapeDtypeStruct((kept, rows, width), jnp.float32),
        in_specs=[smem, smem, smem, vmem, pl.BlockSpec(memory_space=pltpu.HBM), vmem],
        out_specs=vmem,
        scratch_shapes=[pltpu.VMEM((requests, rows, width), kind)] * 2 + first + second + third,
        compiler_params=pltpu.CompilerParams(
            collective_id=0, has_side_effects=True, vmem_limit_bytes=52 * 1024 * 1024
        ),
        name="exchange",
    )(table, my_owners, request, dens_tiles, basis_values, weights)


def shards(basis_values, dens_tiles, region_tiles, point_counts, point_weights):
    owner_count = lax.axis_size("region")
    batch_count = lax.axis_size("batch")
    ring = owner_count // COLUMNS
    my_index = lax.axis_index("region")
    region_local = basis_values.shape[0]
    point_local = basis_values.shape[2]
    tile_local = dens_tiles.shape[0]
    requests = 3 * region_local
    owners = region_tiles.reshape(owner_count, requests) // tile_local
    local_ids = region_tiles.reshape(owner_count, requests) % tile_local
    mine = owners[:, :, None] == jnp.arange(owner_count, dtype=jnp.int32)
    wanted = jnp.sum(jnp.where(mine, local_ids[:, :, None] + 1, 0), axis=1) - 1
    order = jnp.arange(requests, dtype=jnp.int32)
    request_of = jnp.sum(jnp.where(mine, order[None, :, None], 0), axis=1)
    my_owners = lax.dynamic_index_in_dim(owners, my_index, 0, keepdims=False)
    request = lax.dynamic_index_in_dim(request_of, my_index, 0, keepdims=False)
    request = request.reshape(COLUMNS, ring)
    table = wanted.reshape(COLUMNS, ring, COLUMNS, ring)
    table = lax.dynamic_index_in_dim(table, my_index % ring, 1, keepdims=False)
    table = lax.dynamic_index_in_dim(table, my_index // ring, 1, keepdims=False)
    live = jnp.arange(point_local, dtype=jnp.int32)[None, :] < point_counts
    weights = jnp.where(live, point_weights, 0.0)[:, :, None]
    return exchange(
        table, my_owners, request, dens_tiles, basis_values, weights, ring, batch_count
    )


def solution(mesh):
    return jax.shard_map(
        shards,
        mesh=mesh,
        in_specs=(
            P("region", None, "batch", None),
            P("region", "batch", None),
            P(),
            P("region", "batch"),
            P("region", "batch"),
        ),
        out_specs=P("region", "batch", None),
        check_vma=False,
    )
```
